32 devices in a mesh: dp: 8 (over z, y), tensor: 4 (over x, core).
Axes of the slice: x: 2, y: 2, z: 4, core: 2. Of those that a mesh axis runs over, the one named last changes fastest.
Arguments:
- block_input: bfloat16 [8192, 768], P(('dp', 'tensor')), may hold values from -6 to 6
- output_grad: bfloat16 [8192, 768], P(('dp', 'tensor')), may hold values from -6 to 6
- segment_ids: int32 [8, 1024], P('dp'), may hold values from 0 to 3, as said below
- positions: int32 [8, 1024], P('dp'), may hold values from 0 to 639, as said below
- gain_one: float32 [768], replicated, may hold values from 0.5 to 1.5
- gain_two: float32 [768], replicated, may hold values from 0.5 to 1.5
- qkv_weight: bfloat16 [768, 3, 768], P(None, None, 'tensor')
- proj_weight: bfloat16 [768, 768], P('tensor'), may hold values from -0.875 to 0.875
- wide_weight: bfloat16 [768, 2, 1152], P(None, None, 'tensor'), may hold values from -0.21875 to 0.21875
- down_weight: bfloat16 [1152, 768], P('tensor'), may hold values from -0.1875 to 0.1875
Outputs:
- block_output: bfloat16 [8192, 768], P(('dp', 'tensor'))
- grad_input: float32 [8192, 768], P(('dp', 'tensor'))
- grad_qkv: float32 [768, 3, 768], P('dp', None, 'tensor')
- grad_proj: float32 [768, 768], P('tensor', 'dp')
- grad_wide: float32 [768, 2, 1152], P('dp', None, 'tensor')
- grad_down: float32 [1152, 768], P('tensor', 'dp')
- grad_gains: float32 [2, 768], replicated
The draws below stay inside these ranges and needn't reach their ends.
Inputs may be any that keep to these rules, and one draw needn't show every extreme that they name: `segment_ids`: in each row the ids never fall and name 4 documents, each of 128 positions or more; some row has a document of 1024 - 3 * (128) positions. `positions`: each token's place within its document: 0 at a document's first token, rising by one.
All inputs are finite; a program needn't handle non-finite values.
Results may differ from the reference program's by a relative error of at most 0.014.
Values may be sent and summed in bfloat16 or wider, within the bound.
No kernel may reach another device: no remote copies, remote signals or barrier semaphores. Data moves between devices by JAX's collectives and lax.ppermute only.
A program may use at most 128 MiB of HBM per device.

```python
import math
import jax
import jax.numpy as jnp
from jax import lax

D = 768
HEADS = 12
HD = 64
FF = 1152
LEN = 1024
DOCS = 4
SEQS = 8
TOKENS = 8192


def document_starts(base_key):
    doc_key = jax.random.fold_in(base_key, 11)
    shortest = LEN // 8
    cut_points = jnp.sort(jax.random.randint(doc_key, (SEQS, DOCS - 1), 0, LEN - DOCS * shortest + 1), axis=1)
    first_row = (jnp.arange(SEQS, dtype=jnp.int32) == 0)[:, None]
    cut_points = jnp.where(first_row, 0, cut_points).astype(jnp.int32)
    return (cut_points + shortest * jnp.arange(1, DOCS, dtype=jnp.int32)[None, :]).astype(jnp.int32)


def draw_segment_ids(key, part):
    starts_all = document_starts(key)
    places = jnp.arange(LEN, dtype=jnp.int32)
    reached = (places[None, None, :] >= starts_all[:, :, None]).astype(jnp.int32)
    return jnp.sum(reached, axis=1).astype(jnp.int32)


def draw_positions(key, part):
    starts_all = document_starts(key)
    places = jnp.arange(LEN, dtype=jnp.int32)
    reached = places[None, None, :] >= starts_all[:, :, None]
    begins = jnp.max(jnp.where(reached, starts_all[:, :, None], 0), axis=1)
    return (places[None, :] - begins).astype(jnp.int32)


def draw_qkv_weight(key, part):
    first_key = jax.random.fold_in(jax.random.fold_in(key, 23), 0)
    base_weight = jax.random.normal(first_key, (D, 3, D), jnp.float32) / math.sqrt(D)
    return base_weight.astype(jnp.bfloat16)


def block_scale(key, extent, cuts, smallest, largest):
    def one(axis_at, blocks):
        heights = jax.random.uniform(jax.random.fold_in(jax.random.fold_in(key, 6), axis_at), (blocks,), jnp.float32, smallest / len(cuts), largest / len(cuts))
        return jnp.repeat(jnp.exp(heights), extent[axis_at] // blocks).reshape((-1,) + (1,) * (len(extent) - axis_at - 1))

    factor_of = one(*cuts[0])
    for cut in cuts[1:]:
        factor_of = factor_of * one(*cut)
    return factor_of


def noise(own_key, shape, deviation, limit, cuts=(), kind=jnp.bfloat16):
    entries = deviation * jax.random.normal(own_key, shape, jnp.float32)
    if cuts:
        entries = entries * block_scale(own_key, shape, cuts, -0.22, 0.18)
    return jnp.clip(entries, -limit, limit).astype(kind)


def setup_inputs(seed: int = 0) -> dict:
    keys = jax.random.split(jax.random.key(seed), 11)
    block_input = noise(keys[0], (TOKENS, D), 1.0, 6.0, ((0, 32),))
    output_grad = noise(keys[1], (TOKENS, D), 1.0, 6.0, ((0, 32),))
    segment_ids = draw_segment_ids(jax.random.fold_in(keys[10], 71), 0)
    positions = draw_positions(jax.random.fold_in(keys[10], 71), 0)
    gain_one = jnp.clip(1.0 + 0.1 * jax.random.normal(keys[4], (D,), jnp.float32), 0.5, 1.5)
    gain_two = jnp.clip(1.0 + 0.1 * jax.random.normal(keys[5], (D,), jnp.float32), 0.5, 1.5)
    qkv_weight = draw_qkv_weight(jax.random.fold_in(keys[10], 71), 0)
    proj_weight = noise(keys[7], (D, D), (D // 16) ** -0.5, 0.875, ((0, 4),))
    wide_weight = noise(keys[8], (D, 2, FF), D ** -0.5, 0.21875, ((2, 4),))
    down_weight = noise(keys[9], (FF, D), FF ** -0.5, 0.1875, ((0, 4),))
    return {"block_input": block_input, "output_grad": output_grad, "segment_ids": segment_ids, "positions": positions, "gain_one": gain_one, "gain_two": gain_two, "qkv_weight": qkv_weight, "proj_weight": proj_weight, "wide_weight": wide_weight, "down_weight": down_weight}


NORM_EPSILON = 1e-05
ROPE_THETA = 160000.0
MASK_FLOOR = -1e+30

def layer_norm(values_in, gain_in):
    average = lax.optimization_barrier(jnp.mean(values_in, axis=-1, keepdims=True))
    centred = values_in - average
    spread = lax.optimization_barrier(jnp.mean(centred * centred, axis=-1, keepdims=True))
    return centred * lax.rsqrt(spread + NORM_EPSILON) * gain_in

def rotary_tables(places, head_size):
    half_size = head_size // 2
    inverse = ROPE_THETA ** (-(2.0 * jnp.arange(half_size, dtype=jnp.float32)) / head_size)
    angles = places.astype(jnp.float32)[:, None] * inverse[None, :]
    cosine_table = jnp.cos(angles)
    sine_table = jnp.sin(angles)
    return (jnp.concatenate([cosine_table, cosine_table], -1), jnp.concatenate([sine_table, sine_table], -1))

def rotate(values_in, cosine_table, sine_table):
    half_size = values_in.shape[-1] // 2
    turned = jnp.concatenate([-values_in[..., half_size:], values_in[..., :half_size]], -1)
    return values_in * cosine_table[:, None, :] + turned * sine_table[:, None, :]

def rotate_back(grads_in, cosine_table, sine_table):
    half_size = grads_in.shape[-1] // 2
    scaled = grads_in * sine_table[:, None, :]
    turned = jnp.concatenate([scaled[..., half_size:], -scaled[..., :half_size]], -1)
    return grads_in * cosine_table[:, None, :] + turned

def gated_gelu(inner):
    return jax.nn.gelu(inner[:, 0], approximate=False) * inner[:, 1]

def tile_scores(query_tile, key_heads, tile_seg, segment, score_scale):
    scores = jnp.einsum('qhe,khe->hqk', query_tile.astype(jnp.float32), key_heads.astype(jnp.float32)) * score_scale
    return jnp.where((tile_seg[:, None] == segment[None, :])[None], scores, MASK_FLOOR)

def attend(query, key_heads, value_heads, segment, tile_rows):
    length, head_count, head_size = query.shape
    score_scale = 1.0 / math.sqrt(head_size)

    def attend_tile(tile_index):
        first_row = (tile_index * tile_rows).astype(jnp.int32)
        query_tile = lax.dynamic_slice_in_dim(query, first_row, tile_rows, 0)
        tile_seg = lax.dynamic_slice_in_dim(segment, first_row, tile_rows, 0)
        scores = tile_scores(query_tile, key_heads, tile_seg, segment, score_scale)
        row_max = lax.optimization_barrier(jnp.max(scores, -1, keepdims=True))
        log_total = jnp.log(lax.optimization_barrier(jnp.sum(jnp.exp(scores - row_max), -1, keepdims=True))) + row_max
        attn_probs = jnp.exp(scores - log_total).astype(jnp.bfloat16)
        mixed_out = jnp.einsum('hqk,khe->qhe', attn_probs.astype(jnp.float32), value_heads.astype(jnp.float32))
        return (mixed_out.astype(jnp.bfloat16), log_total[..., 0])
    tile_count = length // tile_rows
    outs, totals = lax.map(attend_tile, jnp.arange(tile_count, dtype=jnp.int32))
    attn_out = outs.reshape(length, head_count, head_size)
    log_totals = jnp.transpose(totals, (1, 0, 2)).reshape(head_count, length)
    return (attn_out, log_totals)

def attend_back(query, key_heads, value_heads, segment, log_totals, grad_attn, row_delta, tile_rows):
    length, head_count, head_size = query.shape
    score_scale = 1.0 / math.sqrt(head_size)

    def back_tile(running, tile_index):
        grad_keys, grad_values = running
        first_row = (tile_index * tile_rows).astype(jnp.int32)
        query_tile = lax.dynamic_slice_in_dim(query, first_row, tile_rows, 0)
        tile_seg = lax.dynamic_slice_in_dim(segment, first_row, tile_rows, 0)
        tile_total = lax.dynamic_slice_in_dim(log_totals, first_row, tile_rows, 1)
        tile_delta = lax.dynamic_slice_in_dim(row_delta, first_row, tile_rows, 1)
        tile_grad = lax.dynamic_slice_in_dim(grad_attn, first_row, tile_rows, 0).astype(jnp.float32)
        scores = tile_scores(query_tile, key_heads, tile_seg, segment, score_scale)
        attn_probs = jnp.exp(scores - tile_total[..., None])
        probs_low = attn_probs.astype(jnp.bfloat16).astype(jnp.float32)
        prob_grads = jnp.einsum('qhe,khe->hqk', tile_grad, value_heads.astype(jnp.float32))
        score_grads = (attn_probs * (prob_grads - tile_delta[..., None])).astype(jnp.bfloat16).astype(jnp.float32)
        grad_rows = score_scale * jnp.einsum('hqk,khe->qhe', score_grads, key_heads.astype(jnp.float32))
        grad_keys = grad_keys + score_scale * jnp.einsum('hqk,qhe->khe', score_grads, query_tile.astype(jnp.float32))
        grad_values = grad_values + jnp.einsum('hqk,qhe->khe', probs_low, tile_grad)
        return ((grad_keys, grad_values), grad_rows)
    empty_grads = jnp.zeros((length, head_count, head_size), jnp.float32)
    tile_count = length // tile_rows
    (grad_keys, grad_values), grad_query = lax.scan(back_tile, (empty_grads, empty_grads), jnp.arange(tile_count, dtype=jnp.int32))
    return (grad_query.reshape(length, head_count, head_size), grad_keys, grad_values)

def sequence_layer(seq_input, seq_grad, segment, places, gain_one, gain_two, qkv_weight, proj_weight, wide_weight, down_weight):
    length = seq_input.shape[0]
    tile_rows = min(512, length)
    head_count = HEADS
    head_size = HD
    resid_in = seq_input.astype(jnp.float32)
    normed_one = layer_norm(resid_in, gain_one).astype(jnp.bfloat16)
    mixed = jnp.einsum('td,dcf->tcf', normed_one.astype(jnp.float32), qkv_weight.astype(jnp.float32))
    cosine_table, sine_table = rotary_tables(places, head_size)
    query = rotate(mixed[:, 0].reshape(length, head_count, head_size), cosine_table, sine_table).astype(jnp.bfloat16)
    key_heads = rotate(mixed[:, 1].reshape(length, head_count, head_size), cosine_table, sine_table).astype(jnp.bfloat16)
    value_heads = mixed[:, 2].reshape(length, head_count, head_size).astype(jnp.bfloat16)
    attn_out, log_totals = attend(query, key_heads, value_heads, segment, tile_rows)
    attn_flat = attn_out.reshape(length, head_count * head_size)
    resid_mid = resid_in + jnp.dot(attn_flat, proj_weight, preferred_element_type=jnp.float32)
    normed_two = layer_norm(resid_mid, gain_two).astype(jnp.bfloat16)
    inner = jnp.einsum('td,dcf->tcf', normed_two.astype(jnp.float32), wide_weight.astype(jnp.float32))
    act = gated_gelu(inner).astype(jnp.bfloat16)
    block_output = (resid_mid + jnp.dot(act, down_weight, preferred_element_type=jnp.float32)).astype(jnp.bfloat16)
    grad_down = jnp.dot(act.T, seq_grad, preferred_element_type=jnp.float32)
    grad_act = jnp.dot(seq_grad, down_weight.T, preferred_element_type=jnp.float32)
    grad_inner = jax.vjp(gated_gelu, inner)[1](grad_act)[0].astype(jnp.bfloat16)
    grad_wide = jnp.einsum('td,tcf->dcf', normed_two.astype(jnp.float32), grad_inner.astype(jnp.float32))
    grad_normed_two = jnp.einsum('tcf,dcf->td', grad_inner.astype(jnp.float32), wide_weight.astype(jnp.float32))
    back_two = jax.vjp(layer_norm, resid_mid, gain_two)[1]
    grad_from_two, grad_gain_two = back_two(grad_normed_two)
    grad_mid = seq_grad.astype(jnp.float32) + grad_from_two
    grad_mid_b = grad_mid.astype(jnp.bfloat16)
    grad_proj = jnp.dot(attn_flat.T, grad_mid_b, preferred_element_type=jnp.float32)
    grad_attn = jnp.dot(grad_mid_b, proj_weight.T, preferred_element_type=jnp.float32).astype(jnp.bfloat16)
    grad_attn = grad_attn.reshape(length, head_count, head_size)
    row_delta = lax.optimization_barrier(jnp.sum(grad_attn.astype(jnp.float32) * attn_out.astype(jnp.float32), -1)).T
    grad_query, grad_keys, grad_values = attend_back(query, key_heads, value_heads, segment, log_totals, grad_attn, row_delta, tile_rows)
    grad_mixed = jnp.stack([rotate_back(grad_query, cosine_table, sine_table).reshape(length, head_count * head_size), rotate_back(grad_keys, cosine_table, sine_table).reshape(length, head_count * head_size), grad_values.reshape(length, head_count * head_size)], axis=1).astype(jnp.bfloat16)
    grad_qkv = jnp.einsum('td,tcf->dcf', normed_one.astype(jnp.float32), grad_mixed.astype(jnp.float32))
    grad_normed_one = jnp.einsum('tcf,dcf->td', grad_mixed.astype(jnp.float32), qkv_weight.astype(jnp.float32))
    back_one = jax.vjp(layer_norm, resid_in, gain_one)[1]
    grad_from_one, grad_gain_one = back_one(grad_normed_one)
    grad_input = grad_mid + grad_from_one
    grad_gains = jnp.stack([grad_gain_one, grad_gain_two])
    return (block_output, grad_input, (grad_qkv, grad_proj, grad_wide, grad_down, grad_gains))

def reference(block_input, output_grad, segment_ids, positions, gain_one, gain_two, qkv_weight, proj_weight, wide_weight, down_weight):
    seq_count = segment_ids.shape[0]
    length = segment_ids.shape[1]
    width = block_input.shape[1]
    inputs_seq = block_input.reshape(seq_count, length, width)
    grads_seq = output_grad.reshape(seq_count, length, width)

    def per_sequence(running, per_seq):
        block_output, grad_input, weight_grads = sequence_layer(per_seq[0], per_seq[1], per_seq[2], per_seq[3], gain_one, gain_two, qkv_weight, proj_weight, wide_weight, down_weight)
        running = tuple((total_grad + new_grad for total_grad, new_grad in zip(running, weight_grads)))
        return (running, (block_output, grad_input))
    empty_sums = (jnp.zeros(qkv_weight.shape, jnp.float32), jnp.zeros(proj_weight.shape, jnp.float32), jnp.zeros(wide_weight.shape, jnp.float32), jnp.zeros(down_weight.shape, jnp.float32), jnp.zeros((2, width), jnp.float32))
    sums_out, (outputs, grad_inputs) = lax.scan(per_sequence, empty_sums, (inputs_seq, grads_seq, segment_ids, positions))
    return (outputs.reshape(seq_count * length, width), grad_inputs.reshape(seq_count * length, width), sums_out[0], sums_out[1], sums_out[2], sums_out[3], sums_out[4])
```

```python
import math

import jax
import jax.numpy as jnp
from jax import lax
from jax.sharding import PartitionSpec as P

HD = 64


NORM_EPSILON = 1e-05
ROPE_THETA = 160000.0
MASK_FLOOR = -1e30


def layer_norm(values_in, gain_in):
    average = jnp.mean(values_in, axis=-1, keepdims=True)
    centred = values_in - average
    spread = jnp.mean(centred * centred, axis=-1, keepdims=True)
    return centred * lax.rsqrt(spread + NORM_EPSILON) * gain_in


def rotary_tables(places, head_size):
    half_size = head_size // 2
    inverse = ROPE_THETA ** (-(2.0 * jnp.arange(half_size, dtype=jnp.float32)) / head_size)
    angles = places.astype(jnp.float32)[:, None] * inverse[None, :]
    cosine_table = jnp.cos(angles)
    sine_table = jnp.sin(angles)
    return (
        jnp.concatenate([cosine_table, cosine_table], -1),
        jnp.concatenate([sine_table, sine_table], -1),
    )


def rotate(values_in, cosine_table, sine_table):
    half_size = values_in.shape[-1] // 2
    turned = jnp.concatenate([-values_in[..., half_size:], values_in[..., :half_size]], -1)
    return values_in * cosine_table[:, None, :] + turned * sine_table[:, None, :]


def rotate_back(grads_in, cosine_table, sine_table):
    half_size = grads_in.shape[-1] // 2
    scaled = grads_in * sine_table[:, None, :]
    turned = jnp.concatenate([scaled[..., half_size:], -scaled[..., :half_size]], -1)
    return grads_in * cosine_table[:, None, :] + turned


def gated_gelu(inner):
    return jax.nn.gelu(inner[:, 0], approximate=False) * inner[:, 1]


def tile_scores(query_tile, key_heads, tile_seg, segment, score_scale):
    scores = (
        jnp.einsum("qhe,khe->hqk", query_tile, key_heads, preferred_element_type=jnp.float32)
        * score_scale
    )
    return jnp.where((tile_seg[:, None] == segment[None, :])[None], scores, MASK_FLOOR)


def attend(query, key_heads, value_heads, segment, tile_rows):
    length, head_count, head_size = query.shape
    score_scale = 1.0 / math.sqrt(head_size)

    def attend_tile(tile_index):
        first_row = tile_index * tile_rows
        query_tile = lax.dynamic_slice_in_dim(query, first_row, tile_rows, 0)
        tile_seg = lax.dynamic_slice_in_dim(segment, first_row, tile_rows, 0)
        scores = tile_scores(query_tile, key_heads, tile_seg, segment, score_scale)
        row_max = jnp.max(scores, -1, keepdims=True)
        log_total = jnp.log(jnp.sum(jnp.exp(scores - row_max), -1, keepdims=True)) + row_max
        attn_probs = jnp.exp(scores - log_total).astype(jnp.bfloat16)
        mixed_out = jnp.einsum(
            "hqk,khe->qhe", attn_probs, value_heads, preferred_element_type=jnp.float32
        )
        return (mixed_out.astype(jnp.bfloat16), log_total[..., 0])

    tile_count = length // tile_rows
    outs, totals = lax.map(attend_tile, jnp.arange(tile_count, dtype=jnp.int32))
    attn_out = outs.reshape(length, head_count, head_size)
    log_totals = jnp.transpose(totals, (1, 0, 2)).reshape(head_count, length)
    return (attn_out, log_totals)


def attend_back(
    query, key_heads, value_heads, segment, log_totals, grad_attn, row_delta, tile_rows
):
    length, head_count, head_size = query.shape
    score_scale = 1.0 / math.sqrt(head_size)

    def back_tile(running, tile_index):
        grad_keys, grad_values = running
        first_row = tile_index * tile_rows
        query_tile = lax.dynamic_slice_in_dim(query, first_row, tile_rows, 0)
        tile_seg = lax.dynamic_slice_in_dim(segment, first_row, tile_rows, 0)
        tile_total = lax.dynamic_slice_in_dim(log_totals, first_row, tile_rows, 1)
        tile_delta = lax.dynamic_slice_in_dim(row_delta, first_row, tile_rows, 1)
        tile_grad = lax.dynamic_slice_in_dim(grad_attn, first_row, tile_rows, 0)
        scores = tile_scores(query_tile, key_heads, tile_seg, segment, score_scale)
        attn_probs = jnp.exp(scores - tile_total[..., None])
        probs_low = attn_probs.astype(jnp.bfloat16)
        prob_grads = jnp.einsum(
            "qhe,khe->hqk", tile_grad, value_heads, preferred_element_type=jnp.float32
        )
        score_grads = (attn_probs * (prob_grads - tile_delta[..., None])).astype(jnp.bfloat16)
        grad_rows = score_scale * jnp.einsum(
            "hqk,khe->qhe", score_grads, key_heads, preferred_element_type=jnp.float32
        )
        grad_keys = grad_keys + score_scale * jnp.einsum(
            "hqk,qhe->khe", score_grads, query_tile, preferred_element_type=jnp.float32
        )
        grad_values = grad_values + jnp.einsum(
            "hqk,qhe->khe", probs_low, tile_grad, preferred_element_type=jnp.float32
        )
        return ((grad_keys, grad_values), grad_rows)

    empty_grads = jnp.zeros((length, head_count, head_size), jnp.float32)
    tile_count = length // tile_rows
    (grad_keys, grad_values), grad_query = lax.scan(
        back_tile, (empty_grads, empty_grads), jnp.arange(tile_count, dtype=jnp.int32)
    )
    return (grad_query.reshape(length, head_count, head_size), grad_keys, grad_values)


def bits_of(axis):
    return range(int(math.log2(lax.axis_size(axis))))


def swap(values_in, axis, bit):
    size = lax.axis_size(axis)
    return lax.ppermute(values_in, axis, [(i, i ^ (1 << bit)) for i in range(size)])


def gather_parts(rows):
    parts = [rows]
    found = {0: rows}
    for bit in reversed(bits_of("tensor")):
        for place in list(found):
            found[place | 1 << bit] = swap(found[place], "tensor", bit)
    return [found[place] for place in range(len(found))]


def scatter_parts(parts):
    left = dict(enumerate(parts))
    for bit in bits_of("tensor"):
        away = [place for place in left if place >> bit & 1]
        sent = jnp.concatenate([left[place].astype(jnp.bfloat16) for place in away], 0)
        came = jnp.split(swap(sent, "tensor", bit), len(away), 0)
        kept = {}
        for place, piece in zip(away, came):
            other = place ^ (1 << bit)
            kept[other] = left[other] + piece.astype(jnp.float32)
        left = kept
    return left[0]


def scatter_rows(total):
    own = lax.axis_index("dp")
    block = total.shape[0] // lax.axis_size("dp")
    for bit in bits_of("dp"):
        mine = own >> bit & 1
        pairs = total.reshape(-1, 2, block, total.shape[-1])
        away = lax.dynamic_index_in_dim(pairs, 1 - mine, 1, keepdims=False)
        kept = lax.dynamic_index_in_dim(pairs, mine, 1, keepdims=False)
        came = swap(away.astype(jnp.bfloat16), "dp", bit)
        total = (kept + came.astype(jnp.float32)).reshape(-1, total.shape[-1])
    return total


def reorder(vector):
    count = lax.axis_size("tensor")
    blocks = vector.reshape(count, -1)
    return blocks[jnp.arange(count) ^ lax.axis_index("tensor")].reshape(-1)


def sum_everywhere(values_in):
    for axis in ("dp", "tensor"):
        for bit in bits_of(axis):
            values_in = values_in + swap(values_in, axis, bit)
    return values_in


def per_device(
    block_input,
    output_grad,
    segment_ids,
    positions,
    gain_one,
    gain_two,
    qkv_weight,
    proj_weight,
    wide_weight,
    down_weight,
):
    length = segment_ids.shape[1]
    tile_rows = min(512, length)
    head_size = HD
    own_rows, width = block_input.shape
    local_width = proj_weight.shape[0]
    head_count = local_width // head_size
    units = down_weight.shape[0]
    count = lax.axis_size("tensor")
    segment = reorder(segment_ids[0])
    places = reorder(positions[0])
    resid_in = block_input.astype(jnp.float32)
    normed_one = layer_norm(resid_in, gain_one).astype(jnp.bfloat16)
    full_one = jnp.concatenate(gather_parts(normed_one), 0)
    full_one, output_grad_late = lax.optimization_barrier((full_one, output_grad))
    full_grad = jnp.concatenate(gather_parts(output_grad_late), 0)
    mixed = jnp.einsum("td,dcf->tcf", full_one, qkv_weight, preferred_element_type=jnp.float32)
    cosine_table, sine_table = rotary_tables(places, head_size)
    query = rotate(
        mixed[:, 0].reshape(length, head_count, head_size), cosine_table, sine_table
    ).astype(jnp.bfloat16)
    key_heads = rotate(
        mixed[:, 1].reshape(length, head_count, head_size), cosine_table, sine_table
    ).astype(jnp.bfloat16)
    value_heads = mixed[:, 2].reshape(length, head_count, head_size).astype(jnp.bfloat16)
    attn_out, log_totals = attend(query, key_heads, value_heads, segment, tile_rows)
    attn_flat = attn_out.reshape(length, local_width)
    resid_mid = resid_in + scatter_parts(
        jnp.split(jnp.dot(attn_flat, proj_weight, preferred_element_type=jnp.float32), count, 0)
    )
    normed_two = layer_norm(resid_mid, gain_two).astype(jnp.bfloat16)
    full_two = jnp.concatenate(gather_parts(normed_two), 0)
    inner = jnp.einsum("td,dcf->tcf", full_two, wide_weight, preferred_element_type=jnp.float32)
    act = gated_gelu(inner).astype(jnp.bfloat16)
    grad_act = lax.dot_general(
        full_grad, down_weight, (((1,), (1,)), ((), ())), preferred_element_type=jnp.float32
    )
    grad_inner = jax.vjp(gated_gelu, inner)[1](grad_act)[0].astype(jnp.bfloat16)
    grad_normed_two = scatter_parts(
        jnp.split(
            jnp.einsum("tcf,dcf->td", grad_inner, wide_weight, preferred_element_type=jnp.float32),
            count,
            0,
        )
    )
    grad_normed_two, act, full_two, grad_inner = lax.optimization_barrier(
        (grad_normed_two, act, full_two, grad_inner)
    )
    back_two = jax.vjp(layer_norm, resid_mid, gain_two)[1]
    grad_mid = output_grad.astype(jnp.float32) + back_two(grad_normed_two)[0]
    grad_mid_b = grad_mid.astype(jnp.bfloat16)
    full_mid = jnp.concatenate(gather_parts(grad_mid_b), 0)
    full_mid, act = lax.optimization_barrier((full_mid, act))
    block_output = (
        resid_mid
        + scatter_parts(
            jnp.split(jnp.dot(act, down_weight, preferred_element_type=jnp.float32), count, 0)
        )
    ).astype(jnp.bfloat16)
    grad_down = lax.dot_general(
        full_grad, act, (((0,), (0,)), ((), ())), preferred_element_type=jnp.float32
    )
    grad_wide = lax.dot_general(
        full_two,
        grad_inner.reshape(length, 2 * units),
        (((0,), (0,)), ((), ())),
        preferred_element_type=jnp.float32,
    )
    gain_part_two = jnp.sum(grad_wide * wide_weight.reshape(width, -1), -1) / gain_two
    sent_wide = scatter_rows(grad_wide)
    sent_down = scatter_rows(grad_down).T
    grad_proj = lax.dot_general(
        full_mid, attn_flat, (((0,), (0,)), ((), ())), preferred_element_type=jnp.float32
    )
    sent_proj = scatter_rows(grad_proj).T
    grad_attn = lax.dot_general(
        full_mid, proj_weight, (((1,), (1,)), ((), ())), preferred_element_type=jnp.float32
    )
    grad_attn = grad_attn.astype(jnp.bfloat16).reshape(length, head_count, head_size)
    row_delta = jnp.sum(grad_attn.astype(jnp.float32) * attn_out.astype(jnp.float32), -1).T
    grad_query, grad_keys, grad_values = attend_back(
        query, key_heads, value_heads, segment, log_totals, grad_attn, row_delta, tile_rows
    )
    grad_mixed = jnp.concatenate(
        [
            rotate_back(grad_query, cosine_table, sine_table).reshape(length, local_width),
            rotate_back(grad_keys, cosine_table, sine_table).reshape(length, local_width),
            grad_values.reshape(length, local_width),
        ],
        axis=1,
    ).astype(jnp.bfloat16)
    flat_qkv = qkv_weight.reshape(width, 3 * local_width)
    grad_normed_one = scatter_parts(
        jnp.split(
            lax.dot_general(
                grad_mixed,
                flat_qkv,
                (((1,), (1,)), ((), ())),
                preferred_element_type=jnp.float32,
            ),
            count,
            0,
        )
    )
    grad_qkv = lax.dot_general(
        full_one, grad_mixed, (((0,), (0,)), ((), ())), preferred_element_type=jnp.float32
    )
    gain_part_one = jnp.sum(grad_qkv * flat_qkv, -1) / gain_one
    sent_qkv = scatter_rows(grad_qkv)
    back_one = jax.vjp(layer_norm, resid_in, gain_one)[1]
    grad_input = grad_mid + back_one(grad_normed_one)[0]
    grad_gains = sum_everywhere(jnp.stack([gain_part_one, gain_part_two]))
    return (
        block_output,
        grad_input,
        sent_qkv.reshape(-1, 3, local_width),
        sent_proj,
        sent_wide.reshape(-1, 2, units),
        sent_down,
        grad_gains,
    )


def solution(mesh):
    placed = (
        P(("dp", "tensor"), None),
        P(("dp", "tensor"), None),
        P("dp", None),
        P("dp", None),
        P(),
        P(),
        P(None, None, "tensor"),
        P("tensor", None),
        P(None, None, "tensor"),
        P("tensor", None),
    )
    return jax.shard_map(
        per_device,
        mesh=mesh,
        in_specs=placed,
        out_specs=(
            P(("dp", "tensor"), None),
            P(("dp", "tensor"), None),
            P("dp", None, "tensor"),
            P("tensor", "dp"),
            P("dp", None, "tensor"),
            P("tensor", "dp"),
            P(),
        ),
        check_vma=False,
    )
```

```python
import math

import jax
import jax.numpy as jnp
from jax import lax
from jax.experimental import pallas as pl
from jax.experimental.pallas import tpu as pltpu
from jax.sharding import PartitionSpec as P


HD = 64


NORM_EPSILON = 1e-05
ROPE_THETA = 160000.0
MASK_FLOOR = -1e30
TILE = 256
LOW = jnp.bfloat16
WIDE = jnp.float32


def bits_of(axis):
    return range(int(math.log2(lax.axis_size(axis))))


def swap(values_in, axis, bit):
    size = lax.axis_size(axis)
    return lax.ppermute(values_in, axis, [(i, i ^ (1 << bit)) for i in range(size)])


def reorder(vector):
    count = lax.axis_size("tensor")
    blocks = vector.reshape(count, -1)
    return blocks[jnp.arange(count) ^ lax.axis_index("tensor")].reshape(-1)


def sum_everywhere(values_in):
    for axis in ("dp", "tensor"):
        for bit in bits_of(axis):
            values_in = values_in + swap(values_in, axis, bit)
    return values_in


def scatter_rows(total, order):
    left = sorted(order, reverse=True)
    total = total.reshape((2,) * len(left) + total.shape[1:])
    for bit in order:
        axis = left.index(bit)
        away = lax.index_in_dim(total, 1, axis, keepdims=False).astype(LOW)
        kept = lax.index_in_dim(total, 0, axis, keepdims=False)
        came = swap(away, "dp", bit)
        left.remove(bit)
        if left:
            total = kept + came.astype(WIDE)
    return kept, came


def call(kernel, outs, *operands, scalars=0, flops=0, scratch=()):
    spaces = [pl.BlockSpec(memory_space=pltpu.SMEM)] * scalars
    spaces += [pl.BlockSpec(memory_space=pltpu.VMEM)] * (len(operands) - scalars)
    moved = sum(x.size * x.dtype.itemsize for x in operands)
    shapes = [jax.ShapeDtypeStruct(shape, kind) for shape, kind in outs]
    return pl.pallas_call(
        kernel,
        out_shape=shapes,
        in_specs=spaces,
        out_specs=[pl.BlockSpec(memory_space=pltpu.VMEM)] * len(shapes),
        scratch_shapes=[pltpu.VMEM(shape, kind) for shape, kind in scratch],
        compiler_params=pltpu.CompilerParams(vmem_limit_bytes=48 << 20),
        cost_estimate=pl.CostEstimate(flops=flops, bytes_accessed=moved, transcendentals=0),
    )(*operands)


def dot(left, right, left_axis=1, right_axis=0):
    return lax.dot_general(
        left, right, (((left_axis,), (right_axis,)), ((), ())), preferred_element_type=WIDE
    )


def normalise(values_in):
    average = jnp.mean(values_in, axis=-1, keepdims=True)
    centred = values_in - average
    spread = jnp.mean(centred * centred, axis=-1, keepdims=True)
    scale = lax.rsqrt(spread + NORM_EPSILON)
    return centred * scale, scale


def normalise_back(grads_in, hat, scale, gain_in):
    scaled = grads_in * gain_in
    first = jnp.mean(scaled, axis=-1, keepdims=True)
    second = jnp.mean(scaled * hat, axis=-1, keepdims=True)
    return scale * (scaled - first - hat * second)


def qkv_kernel(near_ref, far_ref, gain_ref, turned_ref, cos_ref, sin_ref, normed_ref, out_ref):
    rows = near_ref.shape[0]
    half = HD // 2
    heads = turned_ref.shape[0] // (3 * HD)
    for place, ref in enumerate((near_ref, far_ref)):
        at = slice(place * rows, (place + 1) * rows)
        hat, _ = normalise(ref[...].astype(WIDE))
        normed = (hat * gain_ref[...]).astype(LOW)
        normed_ref[:, at] = normed.T
        mixed = dot(turned_ref[...], normed, 1, 1)
        cosine, sine = cos_ref[:, at], sin_ref[:, at]
        for head in range(2 * heads):
            lower = mixed[head * HD : head * HD + half]
            upper = mixed[head * HD + half : (head + 1) * HD]
            scale = 1.0 / math.sqrt(HD) if head < heads else 1.0
            first = (lower * cosine - upper * sine).astype(LOW)
            second = (upper * cosine + lower * sine).astype(LOW)
            out_ref[head * HD : head * HD + half, at] = first * scale
            out_ref[head * HD + half : (head + 1) * HD, at] = second * scale
        out_ref[2 * heads * HD :, at] = mixed[2 * heads * HD :].astype(LOW)


def attend_kernel(
    near_ref, far_ref, seg_row_ref, seg_col_ref, proj_ref,
    out_ref, total_ref, keep_near_ref, keep_far_ref, away_near_ref, away_far_ref,
    keys_ref, values_ref,
):
    length = seg_row_ref.shape[1]
    half_length = near_ref.shape[1]
    width = proj_ref.shape[0]
    heads = width // HD
    for place, ref in enumerate((near_ref, far_ref)):
        at = slice(place * half_length, (place + 1) * half_length)
        for head in range(heads):
            keys = ref[width + head * HD : width + (head + 1) * HD, :]
            keys_ref[head, at, :] = keys.T
        values_ref[:, at] = ref[2 * width :, :]
    for tile in range(length // TILE):
        ref = near_ref if tile * TILE < half_length else far_ref
        first = (tile * TILE) % half_length
        at = slice(tile * TILE, (tile + 1) * TILE)
        column = jnp.concatenate([seg_col_ref[...]] * (TILE // seg_col_ref.shape[1]), 1)
        same = column == seg_row_ref[:, at]
        for head in range(heads):
            query = ref[head * HD : (head + 1) * HD, first : first + TILE]
            scores = jnp.where(same, dot(keys_ref[head], query), MASK_FLOOR)
            top = jnp.max(scores, 0, keepdims=True)
            raised = jnp.exp(scores - top)
            total = jnp.sum(raised, 0, keepdims=True)
            mixed = dot(values_ref[head * HD : (head + 1) * HD, :], raised.astype(LOW))
            out_ref[head * HD : (head + 1) * HD, at] = (mixed / total).astype(LOW)
            total_ref[head : head + 1, at] = top + jnp.log(total)
    rows = keep_near_ref.shape[0]
    refs = (keep_near_ref, away_near_ref, keep_far_ref, away_far_ref)
    for place, ref in enumerate(refs):
        part = dot(out_ref[:, place * rows : (place + 1) * rows], proj_ref[...], 0, 0)
        ref[...] = part.astype(ref.dtype)


def middle_kernel(x_ref, keep_ref, core_ref, chip_ref, gain_ref, mid_ref, normed_ref):
    total = x_ref[...].astype(WIDE) + keep_ref[...]
    total = total + core_ref[...].astype(WIDE) + chip_ref[...].astype(WIDE)
    mid_ref[...] = total
    normed_ref[...] = (normalise(total)[0] * gain_ref[...]).astype(LOW)


def forward_kernel(
    near_ref, far_ref, grad_near_ref, grad_far_ref, gate_w_ref, up_w_ref, down_ref,
    dgate_ref, dup_ref, act_ref, keep_ref, away_ref,
):
    rows = near_ref.shape[0]
    parts = ((near_ref, grad_near_ref, keep_ref), (far_ref, grad_far_ref, away_ref))
    for place, (ref, grad_ref, part_ref) in enumerate(parts):
        at = slice(place * rows, (place + 1) * rows)
        gate = dot(ref[...], gate_w_ref[...], 1, 1)
        up = dot(ref[...], up_w_ref[...], 1, 1)
        grad_act = dot(grad_ref[...], down_ref[...], 1, 1)
        share = 0.5 * (1.0 + lax.erf(gate * (1.0 / math.sqrt(2.0))))
        bell = jnp.exp(-0.5 * gate * gate) * (1.0 / math.sqrt(2.0 * math.pi))
        curved = gate * share
        act_ref[at, :] = (curved * up).astype(LOW)
        grad_gate = (grad_act * up * (share + gate * bell)).astype(LOW)
        grad_up = (grad_act * curved).astype(LOW)
        dgate_ref[at, :] = grad_gate
        dup_ref[at, :] = grad_up
        part = dot(grad_gate, gate_w_ref[...]) + dot(grad_up, up_w_ref[...])
        part_ref[...] = part.astype(part_ref.dtype)


def middle_back_kernel(
    mid_ref, grad_ref, keep_ref, core_ref, chip_ref, gain_ref, out_ref, low_ref
):
    total = keep_ref[...] + core_ref[...].astype(WIDE) + chip_ref[...].astype(WIDE)
    hat, scale = normalise(mid_ref[...])
    out = grad_ref[...].astype(WIDE) + normalise_back(total, hat, scale, gain_ref[...])
    out_ref[...] = out
    low_ref[...] = out.astype(LOW)


def store_blocks(own_ref, out_ref, total, first):
    blocks, rows, _ = out_ref.shape
    for block in range(blocks):
        place = jnp.bitwise_xor(own_ref[0], block)
        out_ref[place, :, first : first + total.shape[1]] = total[
            block * rows : (block + 1) * rows
        ]


def wide_grad_kernel(
    own_ref, n0, n1, n2, n3, g0, g1, g2, g3, dgate_a, dgate_b, dup_a, dup_b, act_a, act_b,
    gate_w_ref, up_w_ref, out_ref, gain_ref,
):
    rows = n0.shape[0]
    units = act_a.shape[1]
    sums = [None, None, None]
    for place, (normed, grad) in enumerate(((n0, g0), (n1, g1), (n2, g2), (n3, g3))):
        at = slice(place % 2 * rows, (place % 2 + 1) * rows)
        turned = normed[...].T
        turned_grad = grad[...].T
        for index, left, pair in (
            (0, turned, (dgate_a, dgate_b)),
            (1, turned, (dup_a, dup_b)),
            (2, turned_grad, (act_a, act_b)),
        ):
            more = dot(left, pair[place // 2][at, :])
            sums[index] = more if sums[index] is None else sums[index] + more
    for index in range(3):
        store_blocks(own_ref, out_ref, sums[index], index * units)
    gate_part = jnp.sum(sums[0] * gate_w_ref[...].astype(WIDE).T, 1, keepdims=True)
    up_part = jnp.sum(sums[1] * up_w_ref[...].astype(WIDE).T, 1, keepdims=True)
    gain_ref[...] = gate_part + up_part


def attend_back_kernel(
    near_ref, far_ref, out_ref, total_ref, m0, m1, m2, m3, proj_ref, seg_row_ref, seg_col_ref,
    cos_ref, sin_ref, turned_ref,
    mixed_ref, keep_near_ref, keep_far_ref, away_near_ref, away_far_ref,
    keys_ref, values_ref, grad_ref, grad_keys_ref, grad_values_ref,
):
    length = seg_row_ref.shape[1]
    half_length = near_ref.shape[1]
    rows = m0.shape[0]
    width = proj_ref.shape[0]
    heads = width // HD
    half = HD // 2
    scale = 1.0 / math.sqrt(HD)
    for place, ref in enumerate((m0, m1, m2, m3)):
        grads = dot(proj_ref[...], ref[...], 1, 1)
        grad_ref[:, place * rows : (place + 1) * rows] = grads.astype(LOW)

    def turn_back(total, first, at):
        cosine, sine = cos_ref[:, at], sin_ref[:, at]
        lower, upper = total[:half], total[half:]
        mixed_ref[first : first + half, at] = (lower * cosine + upper * sine).astype(LOW)
        mixed_ref[first + half : first + HD, at] = (upper * cosine - lower * sine).astype(LOW)

    for head in range(heads):
        here = slice(head * HD, (head + 1) * HD)
        for place, ref in enumerate((near_ref, far_ref)):
            at = slice(place * half_length, (place + 1) * half_length)
            keys = ref[width + head * HD : width + (head + 1) * HD, :]
            keys_ref[at, :] = keys.T
            values_ref[at, :] = ref[2 * width + head * HD : 2 * width + (head + 1) * HD, :].T
        for tile in range(length // TILE):
            ref = near_ref if tile * TILE < half_length else far_ref
            first = (tile * TILE) % half_length
            at = slice(tile * TILE, (tile + 1) * TILE)
            column = jnp.concatenate([seg_col_ref[...]] * (TILE // seg_col_ref.shape[1]), 1)
            same = column == seg_row_ref[:, at]
            query = ref[here, first : first + TILE]
            grads = grad_ref[here, at]
            delta = jnp.sum(
                grads.astype(WIDE) * out_ref[here, at].astype(WIDE), 0, keepdims=True
            )
            scores = dot(keys_ref[...], query) - total_ref[head : head + 1, at]
            probs = jnp.exp(jnp.where(same, scores, MASK_FLOOR))
            prob_grads = dot(values_ref[...], grads)
            score_grads = (probs * (prob_grads - delta)).astype(LOW)
            low = probs.astype(LOW)
            grad_query = dot(near_ref[width + head * HD : width + (head + 1) * HD, :],
                             score_grads[:half_length])
            grad_query += dot(far_ref[width + head * HD : width + (head + 1) * HD, :],
                              score_grads[half_length:])
            turn_back(grad_query * scale, head * HD, at)
            more_keys = dot(query, score_grads, 1, 1)
            more_values = dot(grads, low, 1, 1)
            if tile == 0:
                grad_keys_ref[...] = more_keys
                grad_values_ref[...] = more_values
            else:
                grad_keys_ref[...] += more_keys
                grad_values_ref[...] += more_values
        everything = slice(0, length)
        turn_back(grad_keys_ref[...], width + head * HD, everything)
        mixed_ref[2 * width + head * HD : 2 * width + (head + 1) * HD, :] = grad_values_ref[
            ...
        ].astype(LOW)
    refs = (keep_near_ref, away_near_ref, keep_far_ref, away_far_ref)
    for place, ref in enumerate(refs):
        part = dot(mixed_ref[:, place * rows : (place + 1) * rows], turned_ref[...], 0, 0)
        ref[...] = part.astype(ref.dtype)


def qkv_grad_kernel(
    own_ref, normed_a, normed_b, mixed_ref, turned_ref, m0, m1, m2, m3, attn_ref,
    first_ref, second_ref, gain_ref,
):
    rows = m0.shape[0]
    half_length = normed_a.shape[1]
    local = attn_ref.shape[0]
    total = dot(normed_a[...], mixed_ref[:, :half_length], 1, 1)
    total += dot(normed_b[...], mixed_ref[:, half_length:], 1, 1)
    store_blocks(own_ref, first_ref, total[:, : 2 * local], 0)
    store_blocks(own_ref, second_ref, total[:, 2 * local :], 0)
    gain_ref[...] = jnp.sum(total * turned_ref[...].astype(WIDE).T, 1, keepdims=True)
    proj = None
    for place, ref in enumerate((m0, m1, m2, m3)):
        more = dot(ref[...].T, attn_ref[:, place * rows : (place + 1) * rows], 1, 1)
        proj = more if proj is None else proj + more
    store_blocks(own_ref, second_ref, proj, local)


def finish_qkv_kernel(kept_a, came_a, kept_b, came_b, qkv_ref, proj_ref):
    local = proj_ref.shape[0]
    first = kept_a[...] + came_a[...].astype(WIDE)
    second = kept_b[...] + came_b[...].astype(WIDE)
    qkv_ref[0] = first[:, :local]
    qkv_ref[1] = first[:, local:]
    qkv_ref[2] = second[:, :local]
    proj_ref[...] = second[:, local:].T


def finish_wide_kernel(kept, came, wide_ref, down_ref):
    units = down_ref.shape[0]
    total = kept[...] + came[...].astype(WIDE)
    wide_ref[0] = total[:, :units]
    wide_ref[1] = total[:, units : 2 * units]
    down_ref[...] = total[:, 2 * units :].T


def last_kernel(x_ref, mid_ref, keep_ref, core_ref, chip_ref, gain_ref, out_ref):
    total = keep_ref[...] + core_ref[...].astype(WIDE) + chip_ref[...].astype(WIDE)
    hat, scale = normalise(x_ref[...].astype(WIDE))
    out_ref[...] = mid_ref[...] + normalise_back(total, hat, scale, gain_ref[...])


def output_kernel(act_a, act_b, down_ref, keep_near_ref, keep_far_ref, away_near_ref, away_far_ref):
    rows = keep_near_ref.shape[0]
    refs = (keep_near_ref, away_near_ref, keep_far_ref, away_far_ref)
    for place, ref in enumerate(refs):
        act = (act_a, act_b)[place // 2][place % 2 * rows : (place % 2 + 1) * rows, :]
        ref[...] = dot(act, down_ref[...]).astype(ref.dtype)


def reduce_parts(keep_far, away_far, away_near):
    came = swap(away_far, "tensor", 0)
    from_chip = swap((keep_far + came.astype(WIDE)).astype(LOW), "tensor", 1)
    return from_chip, swap(away_near, "tensor", 0)


def per_device(
    block_input,
    output_grad,
    segment_ids,
    positions,
    gain_one,
    gain_two,
    qkv_weight,
    proj_weight,
    wide_weight,
    down_weight,
):
    length = segment_ids.shape[1]
    rows, width = block_input.shape
    local = proj_weight.shape[0]
    heads = local // HD
    units = down_weight.shape[0]
    near = 2 * rows
    blocks = lax.axis_size("dp")
    own = lax.axis_index("dp").reshape(1)
    gain_a = gain_one.reshape(1, width)
    gain_b = gain_two.reshape(1, width)

    x_far = swap(block_input, "tensor", 1)
    x_core = swap(block_input, "tensor", 0)
    segment = reorder(segment_ids[0])
    places = reorder(positions[0])
    seg_row = segment.reshape(1, length)
    seg_col = jnp.broadcast_to(segment[:, None], (length, 128))
    inverse = ROPE_THETA ** (-(2.0 * jnp.arange(HD // 2, dtype=WIDE)) / HD)
    angles = inverse[:, None] * places.astype(WIDE)[None, :]
    cosine, sine = jnp.cos(angles), jnp.sin(angles)
    turned = qkv_weight.reshape(width, 3 * local).T
    gate_w, up_w = wide_weight[:, 0].T, wide_weight[:, 1].T

    qkv_outs = [((width, near), LOW), ((3 * local, near), LOW)]
    qkv_flops = 2 * near * width * 3 * local
    normed_near, mixed_near = call(
        qkv_kernel, qkv_outs, block_input, x_core, gain_a, turned,
        cosine[:, :near], sine[:, :near], flops=qkv_flops,
    )
    x_both = swap(x_far, "tensor", 0)
    normed_far, mixed_far = call(
        qkv_kernel, qkv_outs, x_far, x_both, gain_a, turned,
        cosine[:, near:], sine[:, near:], flops=qkv_flops,
    )
    late, _ = lax.optimization_barrier((output_grad, x_far))
    g_far = swap(late, "tensor", 1)
    g_core = swap(late, "tensor", 0)
    g_both = swap(g_far, "tensor", 0)

    rows_wide, rows_low = ((rows, width), WIDE), ((rows, width), LOW)
    parts_outs = [rows_wide, rows_wide, rows_low, rows_low]
    attn, totals, keep_near, keep_far, away_near, away_far = call(
        attend_kernel,
        [((local, length), LOW), ((heads, length), WIDE)] + parts_outs,
        mixed_near, mixed_far, seg_row, seg_col, proj_weight,
        scratch=[((heads, length, HD), LOW), ((local, length), LOW)],
        flops=16 * heads * length * length * HD,
    )
    from_chip, from_core = reduce_parts(keep_far, away_far, away_near)
    mid, n0 = call(
        middle_kernel, [rows_wide, rows_low],
        block_input, keep_near, from_core, from_chip, gain_b,
    )
    n2 = swap(n0, "tensor", 1)
    n1 = swap(n0, "tensor", 0)
    ff_outs = [((near, units), LOW)] * 3 + [rows_wide, rows_low]
    ff_flops = 2 * near * width * units * 6
    dgate_near, dup_near, act_near, keep_near, away_near = call(
        forward_kernel, ff_outs, n0, n1, output_grad, g_core, gate_w, up_w, down_weight,
        flops=ff_flops,
    )
    n3 = swap(n2, "tensor", 0)
    dgate_far, dup_far, act_far, keep_far, away_far = call(
        forward_kernel, ff_outs, n2, n3, g_far, g_both, gate_w, up_w, down_weight,
        flops=ff_flops,
    )
    from_chip, from_core = reduce_parts(keep_far, away_far, away_near)
    grad_mid, m0 = call(
        middle_back_kernel, [rows_wide, rows_low],
        mid, output_grad, keep_near, from_core, from_chip, gain_b,
    )
    m2 = swap(m0, "tensor", 1)
    m1 = swap(m0, "tensor", 0)
    m3 = swap(m2, "tensor", 0)

    wide_total, gain_part_two = call(
        wide_grad_kernel,
        [((blocks, width // blocks, 3 * units), WIDE), ((width, 1), WIDE)],
        own, n0, n1, n2, n3, output_grad, g_core, g_far, g_both,
        dgate_near, dgate_far, dup_near, dup_far, act_near, act_far, gate_w, up_w,
        scalars=1, flops=2 * length * width * units * 3,
    )
    order = list(bits_of("dp"))
    kept, came = scatter_rows(wide_total, order)
    grad_wide, grad_down = call(
        finish_wide_kernel,
        [((2, width // blocks, units), WIDE), ((units, width // blocks), WIDE)],
        kept, came,
    )

    out_near, out_far, out_away_near, out_away_far = call(
        output_kernel, parts_outs, act_near, act_far, down_weight,
        flops=2 * length * width * units,
    )
    out_chip, out_core = reduce_parts(out_far, out_away_far, out_away_near)
    block_output = (
        mid + out_near + out_core.astype(WIDE) + out_chip.astype(WIDE)
    ).astype(LOW)

    grad_mixed, keep_near, keep_far, away_near, away_far = call(
        attend_back_kernel,
        [((3 * local, length), LOW)] + parts_outs,
        mixed_near, mixed_far, attn, totals, m0, m1, m2, m3, proj_weight, seg_row, seg_col,
        cosine, sine, turned,
        scratch=[((length, HD), LOW), ((length, HD), LOW), ((local, length), LOW),
                 ((HD, length), WIDE), ((HD, length), WIDE)],
        flops=40 * heads * length * length * HD,
    )
    from_chip, from_core = reduce_parts(keep_far, away_far, away_near)
    half_blocks = ((blocks, width // blocks, 2 * local), WIDE)
    first_total, second_total, gain_part_one = call(
        qkv_grad_kernel,
        [half_blocks, half_blocks, ((width, 1), WIDE)],
        own, normed_near, normed_far, grad_mixed, turned, m0, m1, m2, m3, attn,
        scalars=1, flops=2 * length * width * local * 4,
    )
    first = scatter_rows(first_total, order)
    second = scatter_rows(second_total, order[1:] + order[:1])
    grad_qkv, grad_proj = call(
        finish_qkv_kernel,
        [((3, width // blocks, local), WIDE), ((local, width // blocks), WIDE)],
        *first, *second,
    )
    gain_parts = jnp.stack(
        [gain_part_one[:, 0] / gain_one, gain_part_two[:, 0] / gain_two]
    )
    grad_gains = sum_everywhere(gain_parts)
    (grad_input,) = call(
        last_kernel, [rows_wide],
        block_input, grad_mid, keep_near, from_core, from_chip, gain_a,
    )
    return (
        block_output,
        grad_input,
        jnp.transpose(grad_qkv, (1, 0, 2)),
        grad_proj,
        jnp.transpose(grad_wide, (1, 0, 2)),
        grad_down,
        grad_gains,
    )


def solution(mesh):
    placed = (
        P(("dp", "tensor"), None),
        P(("dp", "tensor"), None),
        P("dp", None),
        P("dp", None),
        P(),
        P(),
        P(None, None, "tensor"),
        P("tensor", None),
        P(None, None, "tensor"),
        P("tensor", None),
    )
    return jax.shard_map(
        per_device,
        mesh=mesh,
        in_specs=placed,
        out_specs=(
            P(("dp", "tensor"), None),
            P(("dp", "tensor"), None),
            P("dp", None, "tensor"),
            P("tensor", "dp"),
            P("dp", None, "tensor"),
            P("tensor", "dp"),
            P(),
        ),
        check_vma=False,
    )
```

```python
import functools
import math

import jax
import jax.numpy as jnp
from jax import lax
from jax.experimental import pallas as pl
from jax.experimental.pallas import tpu as pltpu
from jax.sharding import PartitionSpec as P


HD = 64


NORM_EPSILON = 1e-05
ROPE_THETA = 160000.0
MASK_FLOOR = -1e30
TILE = 256
LOW = jnp.bfloat16
WIDE = jnp.float32


def bits_of(axis):
    return range(int(math.log2(lax.axis_size(axis))))


def swap(values_in, axis, bit):
    size = lax.axis_size(axis)
    return lax.ppermute(values_in, axis, [(i, i ^ (1 << bit)) for i in range(size)])


def sum_everywhere(values_in):
    steps = [("dp", bit) for bit in bits_of("dp")]
    steps[1:1] = [("tensor", 0)]
    steps += [("tensor", bit) for bit in bits_of("tensor") if bit]
    for axis, bit in steps:
        values_in = values_in + swap(values_in, axis, bit)
    return values_in


def scatter_rows(kept, away, order):
    left = sorted(order, reverse=True)
    for step, bit in enumerate(order):
        axis = left.index(bit)
        if step:
            total = total.reshape((2,) * len(left) + kept.shape[-2:])
            away = lax.index_in_dim(total, 1, axis, keepdims=False).astype(LOW)
            kept = lax.index_in_dim(total, 0, axis, keepdims=False)
        came = swap(away, "dp", bit)
        left.remove(bit)
        if left:
            total = kept + came.astype(WIDE)
    return kept.reshape(kept.shape[-2:]), came.reshape(kept.shape[-2:])


def call(kernel, outs, *operands, scalars=0, flops=0, scratch=(), limit=20, streamed=False):
    spaces = [pl.BlockSpec(memory_space=pltpu.SMEM)] * scalars
    space = pltpu.HBM if streamed else pltpu.VMEM
    spaces += [pl.BlockSpec(memory_space=space)] * (len(operands) - scalars)
    held = [pltpu.VMEM(shape, kind) for shape, kind in scratch]
    if streamed:
        held += [pltpu.VMEM(x.shape, x.dtype) for x in operands[scalars:]]
        held += [pltpu.SemaphoreType.DMA((len(operands) - scalars,))]
    moved = sum(x.size * x.dtype.itemsize for x in operands)
    shapes = [jax.ShapeDtypeStruct(shape, kind) for shape, kind in outs]
    return pl.pallas_call(
        kernel,
        out_shape=shapes,
        in_specs=spaces,
        out_specs=[pl.BlockSpec(memory_space=pltpu.VMEM)] * len(shapes),
        scratch_shapes=held,
        compiler_params=pltpu.CompilerParams(vmem_limit_bytes=limit << 20),
        cost_estimate=pl.CostEstimate(flops=flops, bytes_accessed=moved, transcendentals=0),
    )(*operands)


def dot(left, right, left_axis=1, right_axis=0):
    return lax.dot_general(
        left, right, (((left_axis,), (right_axis,)), ((), ())), preferred_element_type=WIDE
    )


def normalise(values_in):
    average = jnp.mean(values_in, axis=-1, keepdims=True)
    centred = values_in - average
    spread = jnp.mean(centred * centred, axis=-1, keepdims=True)
    scale = lax.rsqrt(spread + NORM_EPSILON)
    return centred * scale, scale


def normalise_back(grads_in, hat, scale, gain_in):
    scaled = grads_in * gain_in
    first = jnp.mean(scaled, axis=-1, keepdims=True)
    second = jnp.mean(scaled * hat, axis=-1, keepdims=True)
    return scale * (scaled - first - hat * second)


def prepare_kernel(own_ref, segment_ref, places_ref, row_ref, column_ref, cos_ref, sin_ref, *, count):
    half = cos_ref.shape[0]
    rows = row_ref.shape[1] // count
    step = lax.broadcasted_iota(jnp.int32, (half, rows), 0).astype(WIDE)
    inverse = jnp.exp(step * (-math.log(ROPE_THETA) / half))
    for place in range(count):
        start = pl.multiple_of(jnp.bitwise_xor(own_ref[0], place) * rows, rows)
        at = slice(place * rows, (place + 1) * rows)
        segment = segment_ref[:, pl.ds(start, rows)]
        row_ref[:, at] = segment
        column_ref[at, :] = jnp.broadcast_to(segment, (column_ref.shape[1], rows)).T
        angles = inverse * places_ref[:, pl.ds(start, rows)].astype(WIDE)
        cos_ref[:, at] = jnp.cos(angles)
        sin_ref[:, at] = jnp.sin(angles)


def qkv_kernel(
    near_ref, far_ref, gain_ref, turned_ref, cos_ref, sin_ref, turned_normed_ref, normed_ref, out_ref,
    *, offset
):
    rows = near_ref.shape[0]
    half = HD // 2
    heads = turned_ref.shape[0] // (3 * HD)
    for place, ref in enumerate((near_ref, far_ref)):
        at = slice(place * rows, (place + 1) * rows)
        hat, _ = normalise(ref[...].astype(WIDE))
        normed = (hat * gain_ref[...]).astype(LOW)
        normed_ref[at, :] = normed
        turned_normed_ref[:, at] = normed.T
        mixed = dot(turned_ref[...], normed, 1, 1)
        there = slice(offset + place * rows, offset + (place + 1) * rows)
        cosine, sine = cos_ref[:, there], sin_ref[:, there]
        for head in range(2 * heads):
            lower = mixed[head * HD : head * HD + half]
            upper = mixed[head * HD + half : (head + 1) * HD]
            scale = 1.0 / math.sqrt(HD) if head < heads else 1.0
            first = (lower * cosine - upper * sine).astype(LOW)
            second = (upper * cosine + lower * sine).astype(LOW)
            out_ref[head * HD : head * HD + half, at] = first * scale
            out_ref[head * HD + half : (head + 1) * HD, at] = second * scale
        out_ref[2 * heads * HD :, at] = mixed[2 * heads * HD :].astype(LOW)


def attend_kernel(
    near_ref, far_ref, seg_row_ref, seg_col_ref, proj_ref,
    out_ref, total_ref, keep_near_ref, keep_far_ref, away_near_ref, away_far_ref,
    keys_ref, values_ref,
):
    length = seg_row_ref.shape[1]
    half_length = near_ref.shape[1]
    width = proj_ref.shape[0]
    heads = width // HD
    for place, ref in enumerate((near_ref, far_ref)):
        at = slice(place * half_length, (place + 1) * half_length)
        for head in range(heads):
            keys = ref[width + head * HD : width + (head + 1) * HD, :]
            keys_ref[head, at, :] = keys.T
        values_ref[:, at] = ref[2 * width :, :]
    for tile in range(length // TILE):
        ref = near_ref if tile * TILE < half_length else far_ref
        first = (tile * TILE) % half_length
        at = slice(tile * TILE, (tile + 1) * TILE)
        column = jnp.concatenate([seg_col_ref[...]] * (TILE // seg_col_ref.shape[1]), 1)
        same = column == seg_row_ref[:, at]
        for head in range(heads):
            query = ref[head * HD : (head + 1) * HD, first : first + TILE]
            scores = jnp.where(same, dot(keys_ref[head], query), MASK_FLOOR)
            top = jnp.max(scores, 0, keepdims=True)
            raised = jnp.exp(scores - top)
            total = jnp.sum(raised, 0, keepdims=True)
            mixed = dot(values_ref[head * HD : (head + 1) * HD, :], raised.astype(LOW))
            out_ref[head * HD : (head + 1) * HD, at] = (mixed / total).astype(LOW)
            total_ref[head, :, at] = top + jnp.log(total)
    rows = keep_near_ref.shape[0]
    refs = (keep_near_ref, away_near_ref, keep_far_ref, away_far_ref)
    for place, ref in enumerate(refs):
        part = dot(out_ref[:, place * rows : (place + 1) * rows], proj_ref[...], 0, 0)
        ref[...] = part.astype(ref.dtype)


def middle_kernel(x_ref, keep_ref, core_ref, chip_ref, gain_ref, mid_ref, normed_ref):
    total = x_ref[...].astype(WIDE) + keep_ref[...]
    total = total + core_ref[...].astype(WIDE) + chip_ref[...].astype(WIDE)
    mid_ref[...] = total
    normed_ref[...] = (normalise(total)[0] * gain_ref[...]).astype(LOW)


def forward_kernel(
    near_ref, far_ref, grad_near_ref, grad_far_ref, gate_w_ref, up_w_ref, down_ref,
    dgate_ref, dup_ref, act_ref, keep_ref, away_ref, gain_ref,
):
    gain_total = None
    rows = near_ref.shape[0]
    parts = ((near_ref, grad_near_ref, keep_ref), (far_ref, grad_far_ref, away_ref))
    for place, (ref, grad_ref, part_ref) in enumerate(parts):
        at = slice(place * rows, (place + 1) * rows)
        gate = dot(ref[...], gate_w_ref[...], 1, 1)
        up = dot(ref[...], up_w_ref[...], 1, 1)
        grad_act = dot(grad_ref[...], down_ref[...], 1, 1)
        share = 0.5 * (1.0 + lax.erf(gate * (1.0 / math.sqrt(2.0))))
        bell = jnp.exp(-0.5 * gate * gate) * (1.0 / math.sqrt(2.0 * math.pi))
        curved = gate * share
        act_ref[at, :] = (curved * up).astype(LOW)
        grad_gate = (grad_act * up * (share + gate * bell)).astype(LOW)
        grad_up = (grad_act * curved).astype(LOW)
        dgate_ref[at, :] = grad_gate
        dup_ref[at, :] = grad_up
        part = dot(grad_gate, gate_w_ref[...]) + dot(grad_up, up_w_ref[...])
        part_ref[...] = part.astype(part_ref.dtype)
        more = jnp.sum(part * ref[...].astype(WIDE), 0, keepdims=True)
        gain_total = more if gain_total is None else gain_total + more
    gain_ref[...] = gain_total


def middle_back_kernel(
    mid_ref, grad_ref, keep_ref, core_ref, chip_ref, gain_ref, out_ref, low_ref
):
    total = keep_ref[...] + core_ref[...].astype(WIDE) + chip_ref[...].astype(WIDE)
    hat, scale = normalise(mid_ref[...])
    out = grad_ref[...].astype(WIDE) + normalise_back(total, hat, scale, gain_ref[...])
    out_ref[...] = out
    low_ref[...] = out.astype(LOW)


def hold_blocks(total, total_ref):
    blocks, rows, _ = total_ref.shape
    for block in range(blocks):
        total_ref[block] = total[block * rows : (block + 1) * rows]


def store_blocks(own_ref, kept_ref, away_ref, total_ref, bit, top, first):
    half_blocks, rows, _ = kept_ref.shape
    columns = slice(first, first + total_ref.shape[2])
    for index in range(half_blocks):
        place = (index >> bit << (bit + 1)) | (index & ((1 << bit) - 1))
        kept = total_ref[jnp.bitwise_xor(own_ref[0], place)]
        away = total_ref[jnp.bitwise_xor(own_ref[0], place | 1 << bit)]
        kept_ref[index, :, columns] = kept[top : top + rows]
        away_ref[index, :, columns] = away[top : top + rows].astype(LOW)


def wide_grad_kernel(own_ref, *refs, bits):
    count = 14
    kept_a, away_a, kept_b, away_b = refs[count : count + 4]
    total_ref = refs[count + 4]
    held = refs[count + 5 : 2 * count + 5]
    semaphores = refs[2 * count + 5]
    copies = [
        pltpu.make_async_copy(refs[index], held[index], semaphores.at[index])
        for index in range(count)
    ]
    for copy in copies:
        copy.start()
    rows = held[6].shape[0]
    units = held[0].shape[1]
    sums = [None, None, None]
    for place in range(4):
        if place % 2 == 0:
            for copy in copies[3 * (place // 2) : 3 * (place // 2) + 3]:
                copy.wait()
        for copy in copies[6 + 2 * place : 8 + 2 * place]:
            copy.wait()
        at = slice(place % 2 * rows, (place % 2 + 1) * rows)
        turned = held[6 + 2 * place][...].T
        turned_grad = held[7 + 2 * place][...].T
        for index, left in enumerate((turned, turned, turned_grad)):
            more = dot(left, held[3 * (place // 2) + index][at, :])
            sums[index] = more if sums[index] is None else sums[index] + more
    half_rows = kept_a.shape[1]
    for index in range(3):
        hold_blocks(sums[index], total_ref)
        store_blocks(own_ref, kept_a, away_a, total_ref, bits[0], 0, index * units)
        store_blocks(own_ref, kept_b, away_b, total_ref, bits[1], half_rows, index * units)


def attend_back_kernel(
    near_ref, far_ref, out_ref, total_ref, m0, m1, m2, m3, proj_ref, seg_row_ref, seg_col_ref,
    cos_ref, sin_ref, turned_ref, rows_near_ref, rows_far_ref,
    mixed_ref, keep_near_ref, keep_far_ref, away_near_ref, away_far_ref, gain_ref,
    keys_ref, values_ref, grad_ref, grad_keys_ref, grad_values_ref,
):
    length = seg_row_ref.shape[1]
    half_length = near_ref.shape[1]
    rows = m0.shape[0]
    width = proj_ref.shape[0]
    heads = width // HD
    half = HD // 2
    scale = 1.0 / math.sqrt(HD)
    for place, ref in enumerate((m0, m1, m2, m3)):
        grads = dot(proj_ref[...], ref[...], 1, 1)
        grad_ref[:, place * rows : (place + 1) * rows] = grads.astype(LOW)

    def turn_back(total, first, at):
        cosine, sine = cos_ref[:, at], sin_ref[:, at]
        lower, upper = total[:half], total[half:]
        turned_lower = (lower * cosine + upper * sine).astype(LOW)
        turned_upper = (upper * cosine - lower * sine).astype(LOW)
        mixed_ref[pl.ds(first, half), at] = turned_lower
        mixed_ref[pl.ds(pl.multiple_of(first + half, half), half), at] = turned_upper

    def slab(head, first):
        return pl.ds(pl.multiple_of(first + head * HD, HD), HD)

    @pl.loop(0, heads)
    def _(head):
        here, keys_at, values_at = slab(head, 0), slab(head, width), slab(head, 2 * width)
        for place, ref in enumerate((near_ref, far_ref)):
            at = slice(place * half_length, (place + 1) * half_length)
            keys_ref[at, :] = ref[keys_at, :].T
            values_ref[at, :] = ref[values_at, :].T
        for tile in range(length // TILE):
            ref = near_ref if tile * TILE < half_length else far_ref
            first = (tile * TILE) % half_length
            at = slice(tile * TILE, (tile + 1) * TILE)
            column = jnp.concatenate([seg_col_ref[...]] * (TILE // seg_col_ref.shape[1]), 1)
            same = column == seg_row_ref[:, at]
            query = ref[here, first : first + TILE]
            grads = grad_ref[here, at]
            delta = jnp.sum(
                grads.astype(WIDE) * out_ref[here, at].astype(WIDE), 0, keepdims=True
            )
            scores = dot(keys_ref[...], query) - total_ref[head, :, at]
            probs = jnp.exp(jnp.where(same, scores, MASK_FLOOR))
            prob_grads = dot(values_ref[...], grads)
            score_grads = (probs * (prob_grads - delta)).astype(LOW)
            low = probs.astype(LOW)
            grad_query = dot(near_ref[keys_at, :], score_grads[:half_length])
            grad_query += dot(far_ref[keys_at, :], score_grads[half_length:])
            turn_back(grad_query * scale, pl.multiple_of(head * HD, HD), at)
            more_keys = dot(query, score_grads, 1, 1)
            more_values = dot(grads, low, 1, 1)
            if tile == 0:
                grad_keys_ref[...] = more_keys
                grad_values_ref[...] = more_values
            else:
                grad_keys_ref[...] += more_keys
                grad_values_ref[...] += more_values
        turn_back(
            grad_keys_ref[...], pl.multiple_of(width + head * HD, HD), slice(0, length)
        )
        mixed_ref[values_at, :] = grad_values_ref[...].astype(LOW)

    refs = (keep_near_ref, away_near_ref, keep_far_ref, away_far_ref)
    for place, ref in enumerate(refs):
        part = dot(mixed_ref[:, place * rows : (place + 1) * rows], turned_ref[...], 0, 0)
        ref[...] = part.astype(ref.dtype)
        normed = (rows_near_ref, rows_far_ref)[place // 2][
            place % 2 * rows : (place % 2 + 1) * rows, :
        ]
        more = jnp.sum(part * normed.astype(WIDE), 0, keepdims=True)
        gain_total = more if place == 0 else gain_total + more
    gain_ref[...] = gain_total


def qkv_grad_kernel(
    own_ref, normed_a, normed_b, mixed_ref, m0, m1, m2, m3, attn_ref,
    kept_a, away_a, kept_b, away_b, total_ref, *, bits,
):
    rows = m0.shape[0]
    half_length = normed_a.shape[1]
    local = attn_ref.shape[0]
    total = dot(normed_a[...], mixed_ref[:, :half_length], 1, 1)
    total += dot(normed_b[...], mixed_ref[:, half_length:], 1, 1)
    hold_blocks(total[:, : 2 * local], total_ref)
    store_blocks(own_ref, kept_a, away_a, total_ref, bits[0], 0, 0)
    proj = None
    for place, ref in enumerate((m0, m1, m2, m3)):
        more = dot(ref[...].T, attn_ref[:, place * rows : (place + 1) * rows], 1, 1)
        proj = more if proj is None else proj + more
    hold_blocks(jnp.concatenate([total[:, 2 * local :], proj], 1), total_ref)
    store_blocks(own_ref, kept_b, away_b, total_ref, bits[1], 0, 0)


def finish_qkv_kernel(kept_a, came_a, kept_b, came_b, qkv_ref, proj_ref):
    local = proj_ref.shape[0]
    first = kept_a[...] + came_a[...].astype(WIDE)
    second = kept_b[...] + came_b[...].astype(WIDE)
    qkv_ref[0] = first[:, :local]
    qkv_ref[1] = first[:, local:]
    qkv_ref[2] = second[:, :local]
    proj_ref[...] = second[:, local:].T


def finish_wide_kernel(kept_a, came_a, kept_b, came_b, wide_ref, down_ref):
    units = down_ref.shape[0]
    half_rows = kept_a.shape[0]
    for place, (kept, came) in enumerate(((kept_a, came_a), (kept_b, came_b))):
        at = slice(place * half_rows, (place + 1) * half_rows)
        total = kept[...] + came[...].astype(WIDE)
        wide_ref[0, at, :] = total[:, :units]
        wide_ref[1, at, :] = total[:, units : 2 * units]
        down_ref[:, at] = total[:, 2 * units :].T


def last_kernel(x_ref, mid_ref, keep_ref, core_ref, chip_ref, gain_ref, out_ref):
    total = keep_ref[...] + core_ref[...].astype(WIDE) + chip_ref[...].astype(WIDE)
    hat, scale = normalise(x_ref[...].astype(WIDE))
    out_ref[...] = mid_ref[...] + normalise_back(total, hat, scale, gain_ref[...])


def output_kernel(act_a, act_b, down_ref, keep_near_ref, keep_far_ref, away_near_ref, away_far_ref):
    rows = keep_near_ref.shape[0]
    refs = (keep_near_ref, away_near_ref, keep_far_ref, away_far_ref)
    for place, ref in enumerate(refs):
        act = (act_a, act_b)[place // 2][place % 2 * rows : (place % 2 + 1) * rows, :]
        ref[...] = dot(act, down_ref[...]).astype(ref.dtype)


def reduce_parts(keep_far, away_far, away_near):
    came = swap(away_far, "tensor", 0)
    from_chip = swap((keep_far + came.astype(WIDE)).astype(LOW), "tensor", 1)
    return from_chip, swap(away_near, "tensor", 0)


def per_device(
    block_input,
    output_grad,
    segment_ids,
    positions,
    gain_one,
    gain_two,
    qkv_weight,
    proj_weight,
    wide_weight,
    down_weight,
):
    length = segment_ids.shape[1]
    rows, width = block_input.shape
    local = proj_weight.shape[0]
    heads = local // HD
    units = down_weight.shape[0]
    near = 2 * rows
    blocks = lax.axis_size("dp")
    own = lax.axis_index("dp").reshape(1)
    gain_a = gain_one.reshape(1, width)
    gain_b = gain_two.reshape(1, width)

    x_far = swap(block_input, "tensor", 1)
    x_core = swap(block_input, "tensor", 0)
    tables = ((HD // 2, length), WIDE)
    seg_row, seg_col, cosine, sine = call(
        functools.partial(prepare_kernel, count=lax.axis_size("tensor")),
        [((1, length), jnp.int32), ((length, 128), jnp.int32), tables, tables],
        lax.axis_index("tensor").reshape(1), segment_ids, positions,
        scalars=1,
    )
    turned = qkv_weight.reshape(width, 3 * local).T
    gate_w, up_w = wide_weight[:, 0].T, wide_weight[:, 1].T

    qkv_outs = [((width, near), LOW), ((near, width), LOW), ((3 * local, near), LOW)]
    qkv_flops = 2 * near * width * 3 * local
    normed_near, rows_near, mixed_near = call(
        functools.partial(qkv_kernel, offset=0), qkv_outs, block_input, x_core, gain_a, turned,
        cosine, sine, flops=qkv_flops,
    )
    x_both = swap(x_far, "tensor", 0)
    normed_far, rows_far, mixed_far = call(
        functools.partial(qkv_kernel, offset=near), qkv_outs, x_far, x_both, gain_a, turned,
        cosine, sine, flops=qkv_flops,
    )
    late, _ = lax.optimization_barrier((output_grad, x_far))
    g_far = swap(late, "tensor", 1)
    g_core = swap(late, "tensor", 0)
    g_both = swap(g_far, "tensor", 0)

    rows_wide, rows_low = ((rows, width), WIDE), ((rows, width), LOW)
    parts_outs = [rows_wide, rows_wide, rows_low, rows_low]
    attn, totals, keep_near, keep_far, away_near, away_far = call(
        attend_kernel,
        [((local, length), LOW), ((heads, 1, length), WIDE)] + parts_outs,
        mixed_near, mixed_far, seg_row, seg_col, proj_weight,
        scratch=[((heads, length, HD), LOW), ((local, length), LOW)],
        flops=16 * heads * length * length * HD,
    )
    from_chip, from_core = reduce_parts(keep_far, away_far, away_near)
    mid, n0 = call(
        middle_kernel, [rows_wide, rows_low],
        block_input, keep_near, from_core, from_chip, gain_b,
    )
    n2 = swap(n0, "tensor", 1)
    n1 = swap(n0, "tensor", 0)
    gain_row = ((1, width), WIDE)
    ff_outs = [((near, units), LOW)] * 3 + [rows_wide, rows_low, gain_row]
    ff_flops = 2 * near * width * units * 6
    dgate_near, dup_near, act_near, keep_near, away_near, gain_near = call(
        forward_kernel, ff_outs, n0, n1, output_grad, g_core, gate_w, up_w, down_weight,
        flops=ff_flops,
    )
    n3 = swap(n2, "tensor", 0)
    dgate_far, dup_far, act_far, keep_far, away_far, gain_far = call(
        forward_kernel, ff_outs, n2, n3, g_far, g_both, gate_w, up_w, down_weight,
        flops=ff_flops,
    )
    from_chip, from_core = reduce_parts(keep_far, away_far, away_near)
    grad_mid, m0 = call(
        middle_back_kernel, [rows_wide, rows_low],
        mid, output_grad, keep_near, from_core, from_chip, gain_b,
    )
    m2 = swap(m0, "tensor", 1)
    m1 = swap(m0, "tensor", 0)
    m3 = swap(m2, "tensor", 0)

    order = list(bits_of("dp"))
    turned_order = order[1:] + order[:1]
    firsts = (order[0], turned_order[0])
    half_rows = width // blocks // 2
    pieces = (blocks // 2, half_rows, 3 * units)
    kept_a, away_a, kept_b, away_b = call(
        functools.partial(wide_grad_kernel, bits=firsts),
        [(pieces, WIDE), (pieces, LOW), (pieces, WIDE), (pieces, LOW)],
        own, dgate_near, dup_near, act_near, dgate_far, dup_far, act_far,
        n0, output_grad, n1, g_core, n2, g_far, n3, g_both, streamed=True, limit=56,
        scratch=[((blocks, width // blocks, units), WIDE)],
        scalars=1, flops=2 * length * width * units * 3,
    )
    first = scatter_rows(kept_a, away_a, order)
    second = scatter_rows(kept_b, away_b, turned_order)
    grad_wide, grad_down = call(
        finish_wide_kernel,
        [((2, width // blocks, units), WIDE), ((units, width // blocks), WIDE)],
        *first, *second,
    )

    out_near, out_far, out_away_near, out_away_far = call(
        output_kernel, parts_outs, act_near, act_far, down_weight,
        flops=2 * length * width * units,
    )
    out_chip, out_core = reduce_parts(out_far, out_away_far, out_away_near)
    block_output = (
        mid + out_near + out_core.astype(WIDE) + out_chip.astype(WIDE)
    ).astype(LOW)

    grad_mixed, keep_near, keep_far, away_near, away_far, gain_part_one = call(
        attend_back_kernel,
        [((3 * local, length), LOW)] + parts_outs + [gain_row],
        mixed_near, mixed_far, attn, totals, m0, m1, m2, m3, proj_weight, seg_row, seg_col,
        cosine, sine, turned, rows_near, rows_far,
        scratch=[((length, HD), LOW), ((length, HD), LOW), ((local, length), LOW),
                 ((HD, length), WIDE), ((HD, length), WIDE)],
        flops=40 * heads * length * length * HD,
    )
    from_chip, from_core = reduce_parts(keep_far, away_far, away_near)
    pieces = (blocks // 2, width // blocks, 2 * local)
    kept_a, away_a, kept_b, away_b = call(
        functools.partial(qkv_grad_kernel, bits=firsts),
        [(pieces, WIDE), (pieces, LOW), (pieces, WIDE), (pieces, LOW)],
        own, normed_near, normed_far, grad_mixed, m0, m1, m2, m3, attn,
        scalars=1, flops=2 * length * width * local * 4,
        scratch=[((blocks, width // blocks, 2 * local), WIDE)],
    )
    first = scatter_rows(kept_a, away_a, order)
    second = scatter_rows(kept_b, away_b, turned_order)
    grad_qkv, grad_proj = call(
        finish_qkv_kernel,
        [((3, width // blocks, local), WIDE), ((local, width // blocks), WIDE)],
        *first, *second,
    )
    grad_gains = sum_everywhere(
        jnp.concatenate([gain_part_one / gain_a, (gain_near + gain_far) / gain_b], 0)
    )
    (grad_input,) = call(
        last_kernel, [rows_wide],
        block_input, grad_mid, keep_near, from_core, from_chip, gain_a,
    )
    return (
        block_output,
        grad_input,
        jnp.transpose(grad_qkv, (1, 0, 2)),
        grad_proj,
        jnp.transpose(grad_wide, (1, 0, 2)),
        grad_down,
        grad_gains,
    )


def solution(mesh):
    placed = (
        P(("dp", "tensor"), None),
        P(("dp", "tensor"), None),
        P("dp", None),
        P("dp", None),
        P(),
        P(),
        P(None, None, "tensor"),
        P("tensor", None),
        P(None, None, "tensor"),
        P("tensor", None),
    )
    return jax.shard_map(
        per_device,
        mesh=mesh,
        in_specs=placed,
        out_specs=(
            P(("dp", "tensor"), None),
            P(("dp", "tensor"), None),
            P("dp", None, "tensor"),
            P("tensor", "dp"),
            P("dp", None, "tensor"),
            P("tensor", "dp"),
            P(),
        ),
        check_vma=False,
    )
```

```python
import functools
import math

import jax
import jax.numpy as jnp
from jax import lax
from jax.experimental import pallas as pl
from jax.experimental.pallas import tpu as pltpu
from jax.sharding import PartitionSpec as P


HD = 64


NORM_EPSILON = 1e-05
ROPE_THETA = 160000.0
MASK_FLOOR = -1e30
TILE = 256
LOW = jnp.bfloat16
WIDE = jnp.float32


def bits_of(axis):
    return range(int(math.log2(lax.axis_size(axis))))


def exchange(values_in, axis, mask):
    size = lax.axis_size(axis)
    return lax.ppermute(values_in, axis, [(i, i ^ mask) for i in range(size)])


def swap(values_in, axis, bit):
    return exchange(values_in, axis, 1 << bit)


def sum_everywhere(values_in):
    steps = [(axis, bit) for axis in ("tensor", "dp") for bit in bits_of(axis)]
    for axis, bit in steps:
        values_in = values_in + swap(values_in, axis, bit)
    return values_in


def scatter_rows(kept, away, order):
    left = sorted(order, reverse=True)
    for step, bit in enumerate(order):
        axis = left.index(bit)
        if step:
            total = total.reshape((2,) * len(left) + kept.shape[-2:])
            away = lax.index_in_dim(total, 1, axis, keepdims=False).astype(LOW)
            kept = lax.index_in_dim(total, 0, axis, keepdims=False)
        came = swap(away, "dp", bit)
        left.remove(bit)
        if left:
            total = kept + came.astype(WIDE)
    return kept.reshape(kept.shape[-2:]), came.reshape(kept.shape[-2:])


def call(kernel, outs, *operands, scalars=0, flops=0, scratch=(), limit=20, streamed=False):
    spaces = [pl.BlockSpec(memory_space=pltpu.SMEM)] * scalars
    space = pltpu.HBM if streamed else pltpu.VMEM
    spaces += [pl.BlockSpec(memory_space=space)] * (len(operands) - scalars)
    held = [pltpu.VMEM(shape, kind) for shape, kind in scratch]
    if streamed:
        held += [pltpu.VMEM(x.shape, x.dtype) for x in operands[scalars:]]
        held += [pltpu.SemaphoreType.DMA((len(operands) - scalars,))]
    moved = sum(x.size * x.dtype.itemsize for x in operands)
    shapes = [jax.ShapeDtypeStruct(shape, kind) for shape, kind in outs]
    return pl.pallas_call(
        kernel,
        out_shape=shapes,
        in_specs=spaces,
        out_specs=[pl.BlockSpec(memory_space=pltpu.VMEM)] * len(shapes),
        scratch_shapes=held,
        compiler_params=pltpu.CompilerParams(vmem_limit_bytes=limit << 20),
        cost_estimate=pl.CostEstimate(flops=flops, bytes_accessed=moved, transcendentals=0),
    )(*operands)


def dot(left, right, left_axis=1, right_axis=0):
    return lax.dot_general(
        left, right, (((left_axis,), (right_axis,)), ((), ())), preferred_element_type=WIDE
    )


def normalise(values_in):
    average = jnp.mean(values_in, axis=-1, keepdims=True)
    centred = values_in - average
    spread = jnp.mean(centred * centred, axis=-1, keepdims=True)
    scale = lax.rsqrt(spread + NORM_EPSILON)
    return centred * scale, scale


def normalise_back(grads_in, hat, scale, gain_in):
    scaled = grads_in * gain_in
    first = jnp.mean(scaled, axis=-1, keepdims=True)
    second = jnp.mean(scaled * hat, axis=-1, keepdims=True)
    return scale * (scaled - first - hat * second)


def prepare_kernel(own_ref, segment_ref, places_ref, row_ref, column_ref, cos_ref, sin_ref, *, count):
    half = cos_ref.shape[0]
    rows = row_ref.shape[1] // count
    step = lax.broadcasted_iota(jnp.int32, (half, rows), 0).astype(WIDE)
    inverse = jnp.exp(step * (-math.log(ROPE_THETA) / half))
    for place in range(count):
        start = pl.multiple_of(jnp.bitwise_xor(own_ref[0], place) * rows, rows)
        at = slice(place * rows, (place + 1) * rows)
        segment = segment_ref[:, pl.ds(start, rows)]
        row_ref[:, at] = segment
        column_ref[at, :] = jnp.broadcast_to(segment, (column_ref.shape[1], rows)).T
        angles = inverse * places_ref[:, pl.ds(start, rows)].astype(WIDE)
        cos_ref[:, at] = jnp.cos(angles)
        sin_ref[:, at] = jnp.sin(angles)


def qkv_kernel(
    near_ref, far_ref, gain_ref, turned_ref, cos_ref, sin_ref, turned_normed_ref, normed_ref, out_ref,
    *, offset
):
    rows = near_ref.shape[0]
    half = HD // 2
    heads = turned_ref.shape[0] // (3 * HD)
    for place, ref in enumerate((near_ref, far_ref)):
        at = slice(place * rows, (place + 1) * rows)
        hat, _ = normalise(ref[...].astype(WIDE))
        normed = (hat * gain_ref[...]).astype(LOW)
        normed_ref[at, :] = normed
        turned_normed_ref[:, at] = normed.T
        mixed = dot(turned_ref[...], normed, 1, 1)
        there = slice(offset + place * rows, offset + (place + 1) * rows)
        cosine, sine = cos_ref[:, there], sin_ref[:, there]
        for head in range(2 * heads):
            lower = mixed[head * HD : head * HD + half]
            upper = mixed[head * HD + half : (head + 1) * HD]
            scale = 1.0 / math.sqrt(HD) if head < heads else 1.0
            first = (lower * cosine - upper * sine).astype(LOW)
            second = (upper * cosine + lower * sine).astype(LOW)
            out_ref[head * HD : head * HD + half, at] = first * scale
            out_ref[head * HD + half : (head + 1) * HD, at] = second * scale
        out_ref[2 * heads * HD :, at] = mixed[2 * heads * HD :].astype(LOW)


def attend_kernel(
    near_ref, far_ref, seg_row_ref, seg_col_ref,
    out_ref, total_ref, part0_ref, part1_ref, part2_ref, part3_ref,
    keys_ref, values_ref,
):
    length = seg_row_ref.shape[1]
    half_length = near_ref.shape[1]
    width = out_ref.shape[0]
    heads = width // HD
    for place, ref in enumerate((near_ref, far_ref)):
        at = slice(place * half_length, (place + 1) * half_length)
        for head in range(heads):
            keys = ref[width + head * HD : width + (head + 1) * HD, :]
            keys_ref[head, at, :] = keys.T
        values_ref[:, at] = ref[2 * width :, :]
    for tile in range(length // TILE):
        ref = near_ref if tile * TILE < half_length else far_ref
        first = (tile * TILE) % half_length
        at = slice(tile * TILE, (tile + 1) * TILE)
        column = jnp.concatenate([seg_col_ref[...]] * (TILE // seg_col_ref.shape[1]), 1)
        same = column == seg_row_ref[:, at]
        for head in range(heads):
            query = ref[head * HD : (head + 1) * HD, first : first + TILE]
            scores = jnp.where(same, dot(keys_ref[head], query), MASK_FLOOR)
            top = jnp.max(scores, 0, keepdims=True)
            raised = jnp.exp(scores - top)
            total = jnp.sum(raised, 0, keepdims=True)
            mixed = dot(values_ref[head * HD : (head + 1) * HD, :], raised.astype(LOW))
            out_ref[head * HD : (head + 1) * HD, at] = (mixed / total).astype(LOW)
            total_ref[head, :, at] = top + jnp.log(total)
    rows = part0_ref.shape[1]
    for place, ref in enumerate((part0_ref, part1_ref, part2_ref, part3_ref)):
        ref[...] = out_ref[:, place * rows : (place + 1) * rows]


def middle_kernel(x_ref, a0, a1, a2, a3, w0, w1, w2, w3, gain_ref, mid_ref, normed_ref):
    total = x_ref[...].astype(WIDE)
    for attn, weight in ((a0, w0), (a1, w1), (a2, w2), (a3, w3)):
        total = total + dot(attn[...], weight[...], 0, 0)
    mid_ref[...] = total
    normed_ref[...] = (normalise(total)[0] * gain_ref[...]).astype(LOW)


def forward_kernel(
    near_ref, far_ref, grad_near_ref, grad_far_ref, gate_w_ref, up_w_ref, down_ref,
    dgate_ref, dup_ref, act_ref, keep_ref, away_ref, gain_ref,
):
    gain_total = None
    rows = near_ref.shape[0]
    parts = ((near_ref, grad_near_ref, keep_ref), (far_ref, grad_far_ref, away_ref))
    for place, (ref, grad_ref, part_ref) in enumerate(parts):
        at = slice(place * rows, (place + 1) * rows)
        gate = dot(ref[...], gate_w_ref[...], 1, 1)
        up = dot(ref[...], up_w_ref[...], 1, 1)
        grad_act = dot(grad_ref[...], down_ref[...], 1, 1)
        share = 0.5 * (1.0 + lax.erf(gate * (1.0 / math.sqrt(2.0))))
        bell = jnp.exp(-0.5 * gate * gate) * (1.0 / math.sqrt(2.0 * math.pi))
        curved = gate * share
        act_ref[at, :] = (curved * up).astype(LOW)
        grad_gate = (grad_act * up * (share + gate * bell)).astype(LOW)
        grad_up = (grad_act * curved).astype(LOW)
        dgate_ref[at, :] = grad_gate
        dup_ref[at, :] = grad_up
        part = dot(grad_gate, gate_w_ref[...]) + dot(grad_up, up_w_ref[...])
        part_ref[...] = part.astype(part_ref.dtype)
        more = jnp.sum(part * ref[...].astype(WIDE), 0, keepdims=True)
        gain_total = more if gain_total is None else gain_total + more
    gain_ref[...] = gain_total


def middle_back_kernel(
    mid_ref, grad_ref, keep_ref, core_ref, chip_ref, gain_ref, w0, w1, w2, w3,
    out_ref, low_ref, part0_ref, part1_ref, part2_ref, part3_ref,
):
    total = keep_ref[...] + core_ref[...].astype(WIDE) + chip_ref[...].astype(WIDE)
    hat, scale = normalise(mid_ref[...])
    out = grad_ref[...].astype(WIDE) + normalise_back(total, hat, scale, gain_ref[...])
    out_ref[...] = out
    low = out.astype(LOW)
    low_ref[...] = low
    parts = (part0_ref, part1_ref, part2_ref, part3_ref)
    for weight, ref in zip((w0, w1, w2, w3), parts):
        ref[...] = dot(weight[...], low, 1, 1).astype(LOW)


def proj_grad_kernel(
    a0, a1, a2, a3, grad_ref, keep_near_ref, keep_far_ref, away_near_ref, away_far_ref
):
    refs = (keep_near_ref, away_near_ref, keep_far_ref, away_far_ref)
    for attn, ref in zip((a0, a1, a2, a3), refs):
        ref[...] = dot(attn[...], grad_ref[...]).astype(ref.dtype)


def hold_blocks(total, total_ref):
    blocks, rows, _ = total_ref.shape
    for block in range(blocks):
        total_ref[block] = total[block * rows : (block + 1) * rows]


def store_blocks(own_ref, kept_ref, away_ref, total_ref, bit, top, first):
    half_blocks, rows, _ = kept_ref.shape
    columns = slice(first, first + total_ref.shape[2])
    for index in range(half_blocks):
        place = (index >> bit << (bit + 1)) | (index & ((1 << bit) - 1))
        kept = total_ref[jnp.bitwise_xor(own_ref[0], place)]
        away = total_ref[jnp.bitwise_xor(own_ref[0], place | 1 << bit)]
        kept_ref[index, :, columns] = kept[top : top + rows]
        away_ref[index, :, columns] = away[top : top + rows].astype(LOW)


def wide_grad_kernel(own_ref, *refs, bits):
    count = 14
    kept_a, away_a, kept_b, away_b = refs[count : count + 4]
    total_ref = refs[count + 4]
    held = refs[count + 5 : 2 * count + 5]
    semaphores = refs[2 * count + 5]
    copies = [
        pltpu.make_async_copy(refs[index], held[index], semaphores.at[index])
        for index in range(count)
    ]
    for copy in copies:
        copy.start()
    rows = held[6].shape[0]
    units = held[0].shape[1]
    sums = [None, None, None]
    for place in range(4):
        if place % 2 == 0:
            for copy in copies[3 * (place // 2) : 3 * (place // 2) + 3]:
                copy.wait()
        for copy in copies[6 + 2 * place : 8 + 2 * place]:
            copy.wait()
        at = slice(place % 2 * rows, (place % 2 + 1) * rows)
        turned = held[6 + 2 * place][...].T
        turned_grad = held[7 + 2 * place][...].T
        for index, left in enumerate((turned, turned, turned_grad)):
            more = dot(left, held[3 * (place // 2) + index][at, :])
            sums[index] = more if sums[index] is None else sums[index] + more
    half_rows = kept_a.shape[1]
    for index in range(3):
        hold_blocks(sums[index], total_ref)
        store_blocks(own_ref, kept_a, away_a, total_ref, bits[0], 0, index * units)
        store_blocks(own_ref, kept_b, away_b, total_ref, bits[1], half_rows, index * units)


def attend_back_kernel(
    near_ref, far_ref, out_ref, total_ref, g0, g1, g2, g3, seg_row_ref, seg_col_ref,
    cos_ref, sin_ref, turned_ref, rows_near_ref, rows_far_ref,
    mixed_ref, keep_near_ref, keep_far_ref, away_near_ref, away_far_ref, gain_ref,
    keys_ref, values_ref, grad_ref, grad_keys_ref, grad_values_ref,
):
    length = seg_row_ref.shape[1]
    half_length = near_ref.shape[1]
    rows = g0.shape[1]
    width = g0.shape[0]
    heads = width // HD
    half = HD // 2
    scale = 1.0 / math.sqrt(HD)
    for place, ref in enumerate((g0, g1, g2, g3)):
        grad_ref[:, place * rows : (place + 1) * rows] = ref[...]

    def turn_back(total, first, at):
        cosine, sine = cos_ref[:, at], sin_ref[:, at]
        lower, upper = total[:half], total[half:]
        turned_lower = (lower * cosine + upper * sine).astype(LOW)
        turned_upper = (upper * cosine - lower * sine).astype(LOW)
        mixed_ref[pl.ds(first, half), at] = turned_lower
        mixed_ref[pl.ds(pl.multiple_of(first + half, half), half), at] = turned_upper

    def slab(head, first):
        return pl.ds(pl.multiple_of(first + head * HD, HD), HD)

    @pl.loop(0, heads)
    def _(head):
        here, keys_at, values_at = slab(head, 0), slab(head, width), slab(head, 2 * width)
        for place, ref in enumerate((near_ref, far_ref)):
            at = slice(place * half_length, (place + 1) * half_length)
            keys_ref[at, :] = ref[keys_at, :].T
            values_ref[at, :] = ref[values_at, :].T
        for tile in range(length // TILE):
            ref = near_ref if tile * TILE < half_length else far_ref
            first = (tile * TILE) % half_length
            at = slice(tile * TILE, (tile + 1) * TILE)
            column = jnp.concatenate([seg_col_ref[...]] * (TILE // seg_col_ref.shape[1]), 1)
            same = column == seg_row_ref[:, at]
            query = ref[here, first : first + TILE]
            grads = grad_ref[here, at]
            delta = jnp.sum(
                grads.astype(WIDE) * out_ref[here, at].astype(WIDE), 0, keepdims=True
            )
            scores = dot(keys_ref[...], query) - total_ref[head, :, at]
            probs = jnp.exp(jnp.where(same, scores, MASK_FLOOR))
            prob_grads = dot(values_ref[...], grads)
            score_grads = (probs * (prob_grads - delta)).astype(LOW)
            low = probs.astype(LOW)
            grad_query = dot(near_ref[keys_at, :], score_grads[:half_length])
            grad_query += dot(far_ref[keys_at, :], score_grads[half_length:])
            turn_back(grad_query * scale, pl.multiple_of(head * HD, HD), at)
            more_keys = dot(query, score_grads, 1, 1)
            more_values = dot(grads, low, 1, 1)
            if tile == 0:
                grad_keys_ref[...] = more_keys
                grad_values_ref[...] = more_values
            else:
                grad_keys_ref[...] += more_keys
                grad_values_ref[...] += more_values
        turn_back(
            grad_keys_ref[...], pl.multiple_of(width + head * HD, HD), slice(0, length)
        )
        mixed_ref[values_at, :] = grad_values_ref[...].astype(LOW)

    refs = (keep_near_ref, away_near_ref, keep_far_ref, away_far_ref)
    for place, ref in enumerate(refs):
        part = dot(mixed_ref[:, place * rows : (place + 1) * rows], turned_ref[...], 0, 0)
        ref[...] = part.astype(ref.dtype)
        normed = (rows_near_ref, rows_far_ref)[place // 2][
            place % 2 * rows : (place % 2 + 1) * rows, :
        ]
        more = jnp.sum(part * normed.astype(WIDE), 0, keepdims=True)
        gain_total = more if place == 0 else gain_total + more
    gain_ref[...] = gain_total


def qkv_grad_kernel(
    own_ref, normed_a, normed_b, mixed_ref, proj_keep, proj_core, proj_chip,
    kept_a, away_a, kept_b, away_b, total_ref, *, bits,
):
    half_length = normed_a.shape[1]
    local = proj_keep.shape[0]
    total = dot(normed_a[...], mixed_ref[:, :half_length], 1, 1)
    total += dot(normed_b[...], mixed_ref[:, half_length:], 1, 1)
    hold_blocks(total[:, : 2 * local], total_ref)
    store_blocks(own_ref, kept_a, away_a, total_ref, bits[0], 0, 0)
    proj = proj_keep[...] + proj_core[...].astype(WIDE) + proj_chip[...].astype(WIDE)
    hold_blocks(jnp.concatenate([total[:, 2 * local :], proj.T], 1), total_ref)
    store_blocks(own_ref, kept_b, away_b, total_ref, bits[1], 0, 0)


def finish_qkv_kernel(kept_a, came_a, kept_b, came_b, qkv_ref, proj_ref):
    local = proj_ref.shape[0]
    first = kept_a[...] + came_a[...].astype(WIDE)
    second = kept_b[...] + came_b[...].astype(WIDE)
    qkv_ref[0] = first[:, :local]
    qkv_ref[1] = first[:, local:]
    qkv_ref[2] = second[:, :local]
    proj_ref[...] = second[:, local:].T


def finish_wide_kernel(kept_a, came_a, kept_b, came_b, wide_ref, down_ref):
    units = down_ref.shape[0]
    half_rows = kept_a.shape[0]
    for place, (kept, came) in enumerate(((kept_a, came_a), (kept_b, came_b))):
        at = slice(place * half_rows, (place + 1) * half_rows)
        total = kept[...] + came[...].astype(WIDE)
        wide_ref[0, at, :] = total[:, :units]
        wide_ref[1, at, :] = total[:, units : 2 * units]
        down_ref[:, at] = total[:, 2 * units :].T


def last_kernel(x_ref, mid_ref, keep_ref, core_ref, chip_ref, gain_ref, out_ref):
    total = keep_ref[...] + core_ref[...].astype(WIDE) + chip_ref[...].astype(WIDE)
    hat, scale = normalise(x_ref[...].astype(WIDE))
    out_ref[...] = mid_ref[...] + normalise_back(total, hat, scale, gain_ref[...])


def output_kernel(act_a, act_b, down_ref, keep_near_ref, keep_far_ref, away_near_ref, away_far_ref):
    rows = keep_near_ref.shape[0]
    refs = (keep_near_ref, away_near_ref, keep_far_ref, away_far_ref)
    for place, ref in enumerate(refs):
        act = (act_a, act_b)[place // 2][place % 2 * rows : (place % 2 + 1) * rows, :]
        ref[...] = dot(act, down_ref[...]).astype(ref.dtype)


def reduce_parts(keep_far, away_far, away_near):
    came = swap(away_far, "tensor", 0)
    from_chip = swap((keep_far + came.astype(WIDE)).astype(LOW), "tensor", 1)
    return from_chip, swap(away_near, "tensor", 0)


def per_device(
    block_input,
    output_grad,
    segment_ids,
    positions,
    gain_one,
    gain_two,
    qkv_weight,
    proj_weight,
    wide_weight,
    down_weight,
):
    length = segment_ids.shape[1]
    rows, width = block_input.shape
    local = proj_weight.shape[0]
    heads = local // HD
    units = down_weight.shape[0]
    near = 2 * rows
    blocks = lax.axis_size("dp")
    own = lax.axis_index("dp").reshape(1)
    gain_a = gain_one.reshape(1, width)
    gain_b = gain_two.reshape(1, width)

    x_far = swap(block_input, "tensor", 1)
    x_core = swap(block_input, "tensor", 0)
    tables = ((HD // 2, length), WIDE)
    seg_row, seg_col, cosine, sine = call(
        functools.partial(prepare_kernel, count=lax.axis_size("tensor")),
        [((1, length), jnp.int32), ((length, 128), jnp.int32), tables, tables],
        lax.axis_index("tensor").reshape(1), segment_ids, positions,
        scalars=1,
    )
    turned = qkv_weight.reshape(width, 3 * local).T
    gate_w, up_w = wide_weight[:, 0].T, wide_weight[:, 1].T

    qkv_outs = [((width, near), LOW), ((near, width), LOW), ((3 * local, near), LOW)]
    qkv_flops = 2 * near * width * 3 * local
    normed_near, rows_near, mixed_near = call(
        functools.partial(qkv_kernel, offset=0), qkv_outs, block_input, x_core, gain_a, turned,
        cosine, sine, flops=qkv_flops,
    )
    x_both = swap(x_far, "tensor", 0)
    normed_far, rows_far, mixed_far = call(
        functools.partial(qkv_kernel, offset=near), qkv_outs, x_far, x_both, gain_a, turned,
        cosine, sine, flops=qkv_flops,
    )
    w0 = proj_weight
    w2 = swap(w0, "tensor", 1)
    w1 = swap(w0, "tensor", 0)
    w3 = swap(w2, "tensor", 0)
    g_far = swap(output_grad, "tensor", 1)
    g_core = swap(output_grad, "tensor", 0)
    g_both = swap(g_far, "tensor", 0)

    rows_wide, rows_low = ((rows, width), WIDE), ((rows, width), LOW)
    parts_outs = [rows_wide, rows_wide, rows_low, rows_low]
    head_parts = [((local, rows), LOW)] * 4
    attn, totals, a0, b1, b2, b3 = call(
        attend_kernel,
        [((local, length), LOW), ((heads, 1, length), WIDE)] + head_parts,
        mixed_near, mixed_far, seg_row, seg_col,
        scratch=[((heads, length, HD), LOW), ((local, length), LOW)],
        flops=16 * heads * length * length * HD,
    )
    a1 = exchange(b1, "tensor", 1)
    a2 = exchange(b2, "tensor", 2)
    a3 = exchange(b3, "tensor", 3)
    mid, n0 = call(
        middle_kernel, [rows_wide, rows_low],
        block_input, a0, a1, a2, a3, w0, w1, w2, w3, gain_b,
    )
    n2 = swap(n0, "tensor", 1)
    n1 = swap(n0, "tensor", 0)
    gain_row = ((1, width), WIDE)
    ff_outs = [((near, units), LOW)] * 3 + [rows_wide, rows_low, gain_row]
    ff_flops = 2 * near * width * units * 6
    dgate_near, dup_near, act_near, keep_near, away_near, gain_near = call(
        forward_kernel, ff_outs, n0, n1, output_grad, g_core, gate_w, up_w, down_weight,
        flops=ff_flops,
    )
    n3 = swap(n2, "tensor", 0)
    dgate_far, dup_far, act_far, keep_far, away_far, gain_far = call(
        forward_kernel, ff_outs, n2, n3, g_far, g_both, gate_w, up_w, down_weight,
        flops=ff_flops,
    )
    from_chip, from_core = reduce_parts(keep_far, away_far, away_near)
    grad_mid, m0, h0, e1, e2, e3 = call(
        middle_back_kernel, [rows_wide, rows_low] + head_parts,
        mid, output_grad, keep_near, from_core, from_chip, gain_b, w0, w1, w2, w3,
    )
    h1 = exchange(e1, "tensor", 1)
    h2 = exchange(e2, "tensor", 2)
    h3 = exchange(e3, "tensor", 3)
    head_wide, head_low = ((local, width), WIDE), ((local, width), LOW)
    proj_keep, proj_far, proj_away_near, proj_away_far = call(
        proj_grad_kernel, [head_wide, head_wide, head_low, head_low],
        a0, a1, a2, a3, m0, flops=2 * length * width * local,
    )
    proj_chip, proj_core = reduce_parts(proj_far, proj_away_far, proj_away_near)

    order = list(bits_of("dp"))
    turned_order = order[1:] + order[:1]
    firsts = (order[0], turned_order[0])
    half_rows = width // blocks // 2
    pieces = (blocks // 2, half_rows, 3 * units)
    kept_a, away_a, kept_b, away_b = call(
        functools.partial(wide_grad_kernel, bits=firsts),
        [(pieces, WIDE), (pieces, LOW), (pieces, WIDE), (pieces, LOW)],
        own, dgate_near, dup_near, act_near, dgate_far, dup_far, act_far,
        n0, output_grad, n1, g_core, n2, g_far, n3, g_both, streamed=True, limit=52,
        scratch=[((blocks, width // blocks, units), WIDE)],
        scalars=1, flops=2 * length * width * units * 3,
    )
    first = scatter_rows(kept_a, away_a, order)
    second = scatter_rows(kept_b, away_b, turned_order)
    grad_wide, grad_down = call(
        finish_wide_kernel,
        [((2, width // blocks, units), WIDE), ((units, width // blocks), WIDE)],
        *first, *second,
    )

    out_near, out_far, out_away_near, out_away_far = call(
        output_kernel, parts_outs, act_near, act_far, down_weight,
        flops=2 * length * width * units,
    )
    out_chip, out_core = reduce_parts(out_far, out_away_far, out_away_near)
    block_output = (
        mid + out_near + out_core.astype(WIDE) + out_chip.astype(WIDE)
    ).astype(LOW)

    grad_mixed, keep_near, keep_far, away_near, away_far, gain_part_one = call(
        attend_back_kernel,
        [((3 * local, length), LOW)] + parts_outs + [gain_row],
        mixed_near, mixed_far, attn, totals, h0, h1, h2, h3, seg_row, seg_col,
        cosine, sine, turned, rows_near, rows_far,
        scratch=[((length, HD), LOW), ((length, HD), LOW), ((local, length), LOW),
                 ((HD, length), WIDE), ((HD, length), WIDE)],
        flops=40 * heads * length * length * HD,
    )
    from_chip, from_core = reduce_parts(keep_far, away_far, away_near)
    pieces = (blocks // 2, width // blocks, 2 * local)
    kept_a, away_a, kept_b, away_b = call(
        functools.partial(qkv_grad_kernel, bits=firsts),
        [(pieces, WIDE), (pieces, LOW), (pieces, WIDE), (pieces, LOW)],
        own, normed_near, normed_far, grad_mixed, proj_keep, proj_core, proj_chip,
        scalars=1, flops=2 * length * width * local * 4,
        scratch=[((blocks, width // blocks, 2 * local), WIDE)],
    )
    first = scatter_rows(kept_a, away_a, order)
    second = scatter_rows(kept_b, away_b, turned_order)
    grad_qkv, grad_proj = call(
        finish_qkv_kernel,
        [((3, width // blocks, local), WIDE), ((local, width // blocks), WIDE)],
        *first, *second,
    )
    grad_gains = sum_everywhere(
        jnp.concatenate([gain_part_one / gain_a, (gain_near + gain_far) / gain_b], 0)
    )
    (grad_input,) = call(
        last_kernel, [rows_wide],
        block_input, grad_mid, keep_near, from_core, from_chip, gain_a,
    )
    return (
        block_output,
        grad_input,
        jnp.transpose(grad_qkv, (1, 0, 2)),
        grad_proj,
        jnp.transpose(grad_wide, (1, 0, 2)),
        grad_down,
        grad_gains,
    )


def solution(mesh):
    placed = (
        P(("dp", "tensor"), None),
        P(("dp", "tensor"), None),
        P("dp", None),
        P("dp", None),
        P(),
        P(),
        P(None, None, "tensor"),
        P("tensor", None),
        P(None, None, "tensor"),
        P("tensor", None),
    )
    return jax.shard_map(
        per_device,
        mesh=mesh,
        in_specs=placed,
        out_specs=(
            P(("dp", "tensor"), None),
            P(("dp", "tensor"), None),
            P("dp", None, "tensor"),
            P("tensor", "dp"),
            P("dp", None, "tensor"),
            P("tensor", "dp"),
            P(),
        ),
        check_vma=False,
    )
```

```python
import functools
import math

import jax
import jax.numpy as jnp
from jax import lax
from jax.experimental import pallas as pl
from jax.experimental.pallas import tpu as pltpu
from jax.sharding import PartitionSpec as P


HD = 64


NORM_EPSILON = 1e-05
ROPE_THETA = 160000.0
MASK_FLOOR = -1e30
TILE = 256
LOW = jnp.bfloat16
WIDE = jnp.float32


def bits_of(axis):
    return range(int(math.log2(lax.axis_size(axis))))


def exchange(values_in, axis, mask):
    size = lax.axis_size(axis)
    return lax.ppermute(values_in, axis, [(i, i ^ mask) for i in range(size)])


def swap(values_in, axis, bit):
    return exchange(values_in, axis, 1 << bit)


def sum_everywhere(values_in):
    steps = [(axis, bit) for axis in ("tensor", "dp") for bit in bits_of(axis)]
    for axis, bit in steps:
        values_in = values_in + swap(values_in, axis, bit)
    return values_in


def scatter_rows(kept, away, order):
    left = sorted(order, reverse=True)
    for step, bit in enumerate(order):
        axis = left.index(bit)
        if step:
            total = total.reshape((2,) * len(left) + kept.shape[-2:])
            away = lax.index_in_dim(total, 1, axis, keepdims=False).astype(LOW)
            kept = lax.index_in_dim(total, 0, axis, keepdims=False)
        came = swap(away, "dp", bit)
        left.remove(bit)
        if left:
            total = kept + came.astype(WIDE)
    return kept.reshape(kept.shape[-2:]), came.reshape(kept.shape[-2:])


def call(kernel, outs, *operands, scalars=0, flops=0, scratch=(), limit=20):
    spaces = [pl.BlockSpec(memory_space=pltpu.SMEM)] * scalars
    spaces += [pl.BlockSpec(memory_space=pltpu.VMEM)] * (len(operands) - scalars)
    held = [pltpu.VMEM(shape, kind) for shape, kind in scratch]
    moved = sum(x.size * x.dtype.itemsize for x in operands)
    shapes = [jax.ShapeDtypeStruct(shape, kind) for shape, kind in outs]
    return pl.pallas_call(
        kernel,
        out_shape=shapes,
        in_specs=spaces,
        out_specs=[pl.BlockSpec(memory_space=pltpu.VMEM)] * len(shapes),
        scratch_shapes=held,
        compiler_params=pltpu.CompilerParams(vmem_limit_bytes=limit << 20),
        cost_estimate=pl.CostEstimate(flops=flops, bytes_accessed=moved, transcendentals=0),
    )(*operands)


def dot(left, right, left_axis=1, right_axis=0):
    return lax.dot_general(
        left, right, (((left_axis,), (right_axis,)), ((), ())), preferred_element_type=WIDE
    )


def normalise(values_in):
    average = jnp.mean(values_in, axis=-1, keepdims=True)
    centred = values_in - average
    spread = jnp.mean(centred * centred, axis=-1, keepdims=True)
    scale = lax.rsqrt(spread + NORM_EPSILON)
    return centred * scale, scale


def normalise_back(grads_in, hat, scale, gain_in):
    scaled = grads_in * gain_in
    first = jnp.mean(scaled, axis=-1, keepdims=True)
    second = jnp.mean(scaled * hat, axis=-1, keepdims=True)
    return scale * (scaled - first - hat * second)


def prepare_kernel(own_ref, segment_ref, places_ref, row_ref, column_ref, cos_ref, sin_ref, *, count):
    half = cos_ref.shape[0]
    rows = row_ref.shape[1] // count
    step = lax.broadcasted_iota(jnp.int32, (half, rows), 0).astype(WIDE)
    inverse = jnp.exp(step * (-math.log(ROPE_THETA) / half))
    for place in range(count):
        start = pl.multiple_of(jnp.bitwise_xor(own_ref[0], place) * rows, rows)
        at = slice(place * rows, (place + 1) * rows)
        segment = segment_ref[:, pl.ds(start, rows)]
        row_ref[:, at] = segment
        column_ref[at, :] = jnp.broadcast_to(segment, (column_ref.shape[1], rows)).T
        angles = inverse * places_ref[:, pl.ds(start, rows)].astype(WIDE)
        cos_ref[:, at] = jnp.cos(angles)
        sin_ref[:, at] = jnp.sin(angles)


def qkv_kernel(
    near_ref, far_ref, gain_ref, turned_ref, cos_ref, sin_ref, turned_normed_ref, normed_ref, out_ref,
    *, offset
):
    rows = near_ref.shape[0]
    half = HD // 2
    heads = turned_ref.shape[0] // (3 * HD)
    for place, ref in enumerate((near_ref, far_ref)):
        at = slice(place * rows, (place + 1) * rows)
        hat, _ = normalise(ref[...].astype(WIDE))
        normed = (hat * gain_ref[...]).astype(LOW)
        normed_ref[at, :] = normed
        turned_normed_ref[:, at] = normed.T
        mixed = dot(turned_ref[...], normed, 1, 1)
        there = slice(offset + place * rows, offset + (place + 1) * rows)
        cosine, sine = cos_ref[:, there], sin_ref[:, there]
        for head in range(2 * heads):
            lower = mixed[head * HD : head * HD + half]
            upper = mixed[head * HD + half : (head + 1) * HD]
            scale = 1.0 / math.sqrt(HD) if head < heads else 1.0
            first = (lower * cosine - upper * sine).astype(LOW)
            second = (upper * cosine + lower * sine).astype(LOW)
            out_ref[head * HD : head * HD + half, at] = first * scale
            out_ref[head * HD + half : (head + 1) * HD, at] = second * scale
        out_ref[2 * heads * HD :, at] = mixed[2 * heads * HD :].astype(LOW)


def attend_kernel(
    near_ref, far_ref, seg_row_ref, seg_col_ref,
    out_ref, total_ref, part0_ref, part1_ref, part2_ref, part3_ref,
    keys_ref, values_ref,
):
    length = seg_row_ref.shape[1]
    half_length = near_ref.shape[1]
    width = out_ref.shape[0]
    heads = width // HD
    for place, ref in enumerate((near_ref, far_ref)):
        at = slice(place * half_length, (place + 1) * half_length)
        for head in range(heads):
            keys = ref[width + head * HD : width + (head + 1) * HD, :]
            keys_ref[head, at, :] = keys.T
        values_ref[:, at] = ref[2 * width :, :]
    for tile in range(length // TILE):
        ref = near_ref if tile * TILE < half_length else far_ref
        first = (tile * TILE) % half_length
        at = slice(tile * TILE, (tile + 1) * TILE)
        column = jnp.concatenate([seg_col_ref[...]] * (TILE // seg_col_ref.shape[1]), 1)
        same = column == seg_row_ref[:, at]
        for head in range(heads):
            query = ref[head * HD : (head + 1) * HD, first : first + TILE]
            scores = jnp.where(same, dot(keys_ref[head], query), MASK_FLOOR)
            top = jnp.max(scores, 0, keepdims=True)
            raised = jnp.exp(scores - top)
            total = jnp.sum(raised, 0, keepdims=True)
            mixed = dot(values_ref[head * HD : (head + 1) * HD, :], raised.astype(LOW))
            out_ref[head * HD : (head + 1) * HD, at] = (mixed / total).astype(LOW)
            total_ref[head, :, at] = top + jnp.log(total)
    rows = part0_ref.shape[1]
    for place, ref in enumerate((part0_ref, part1_ref, part2_ref, part3_ref)):
        ref[...] = out_ref[:, place * rows : (place + 1) * rows]


def middle_kernel(x_ref, a0, a1, a2, a3, w0, w1, w2, w3, gain_ref, mid_ref, normed_ref):
    total = x_ref[...].astype(WIDE)
    for attn, weight in ((a0, w0), (a1, w1), (a2, w2), (a3, w3)):
        total = total + dot(attn[...], weight[...], 0, 0)
    mid_ref[...] = total
    normed_ref[...] = (normalise(total)[0] * gain_ref[...]).astype(LOW)


def forward_kernel(
    near_ref, far_ref, grad_near_ref, grad_far_ref, gate_w_ref, up_w_ref, down_ref,
    dgate_ref, dup_ref, act_ref, keep_ref, away_ref, gain_ref,
):
    gain_total = None
    rows = near_ref.shape[0]
    parts = ((near_ref, grad_near_ref, keep_ref), (far_ref, grad_far_ref, away_ref))
    for place, (ref, grad_ref, part_ref) in enumerate(parts):
        at = slice(place * rows, (place + 1) * rows)
        gate = dot(ref[...], gate_w_ref[...], 1, 1)
        up = dot(ref[...], up_w_ref[...], 1, 1)
        grad_act = dot(grad_ref[...], down_ref[...], 1, 1)
        share = 0.5 * (1.0 + lax.erf(gate * (1.0 / math.sqrt(2.0))))
        bell = jnp.exp(-0.5 * gate * gate) * (1.0 / math.sqrt(2.0 * math.pi))
        curved = gate * share
        act_ref[at, :] = (curved * up).astype(LOW)
        grad_gate = (grad_act * up * (share + gate * bell)).astype(LOW)
        grad_up = (grad_act * curved).astype(LOW)
        dgate_ref[at, :] = grad_gate
        dup_ref[at, :] = grad_up
        part = dot(grad_gate, gate_w_ref[...]) + dot(grad_up, up_w_ref[...])
        part_ref[...] = part.astype(part_ref.dtype)
        more = jnp.sum(part * ref[...].astype(WIDE), 0, keepdims=True)
        gain_total = more if gain_total is None else gain_total + more
    gain_ref[...] = gain_total


def middle_back_kernel(
    mid_ref, grad_ref, keep_ref, core_ref, chip_ref, gain_ref, w0, w1, w2, w3,
    out_ref, low_ref, part0_ref, part1_ref, part2_ref, part3_ref,
):
    total = keep_ref[...] + core_ref[...].astype(WIDE) + chip_ref[...].astype(WIDE)
    hat, scale = normalise(mid_ref[...])
    out = grad_ref[...].astype(WIDE) + normalise_back(total, hat, scale, gain_ref[...])
    out_ref[...] = out
    low = out.astype(LOW)
    low_ref[...] = low
    parts = (part0_ref, part1_ref, part2_ref, part3_ref)
    for weight, ref in zip((w0, w1, w2, w3), parts):
        ref[...] = dot(weight[...], low, 1, 1).astype(LOW)


def proj_grad_kernel(
    a0, a1, a2, a3, grad_ref, keep_near_ref, keep_far_ref, away_near_ref, away_far_ref
):
    refs = (keep_near_ref, away_near_ref, keep_far_ref, away_far_ref)
    for attn, ref in zip((a0, a1, a2, a3), refs):
        ref[...] = dot(attn[...], grad_ref[...]).astype(ref.dtype)


def hold_blocks(total, total_ref):
    blocks, rows, _ = total_ref.shape
    for block in range(blocks):
        total_ref[block] = total[block * rows : (block + 1) * rows]


def store_blocks(own_ref, kept_ref, away_ref, total_ref, bit, top, first):
    half_blocks, rows, _ = kept_ref.shape
    columns = slice(first, first + total_ref.shape[2])
    for index in range(half_blocks):
        place = (index >> bit << (bit + 1)) | (index & ((1 << bit) - 1))
        kept = total_ref[jnp.bitwise_xor(own_ref[0], place)]
        away = total_ref[jnp.bitwise_xor(own_ref[0], place | 1 << bit)]
        kept_ref[index, :, columns] = kept[top : top + rows]
        away_ref[index, :, columns] = away[top : top + rows].astype(LOW)


def wide_sums(n0, n1, g0, g1, dgate_ref, dup_ref, act_ref):
    rows = n0.shape[0]
    sums = [None, None, None]
    for place, (normed, grad) in enumerate(((n0, g0), (n1, g1))):
        at = slice(place * rows, (place + 1) * rows)
        turned, turned_grad = normed[...].T, grad[...].T
        for index, (left, ref) in enumerate(
            ((turned, dgate_ref), (turned, dup_ref), (turned_grad, act_ref))
        ):
            more = dot(left, ref[at, :])
            sums[index] = more if sums[index] is None else sums[index] + more
    return sums


def wide_near_kernel(n0, n1, g0, g1, dgate_ref, dup_ref, act_ref, out_ref):
    for index, total in enumerate(wide_sums(n0, n1, g0, g1, dgate_ref, dup_ref, act_ref)):
        out_ref[index] = total


def wide_far_kernel(
    own_ref, n0, n1, g0, g1, dgate_ref, dup_ref, act_ref, near_ref,
    kept_a, away_a, kept_b, away_b, total_ref, *, bits,
):
    half_rows = kept_a.shape[1]
    units = act_ref.shape[1]
    for index, total in enumerate(wide_sums(n0, n1, g0, g1, dgate_ref, dup_ref, act_ref)):
        hold_blocks(total + near_ref[index], total_ref)
        store_blocks(own_ref, kept_a, away_a, total_ref, bits[0], 0, index * units)
        store_blocks(own_ref, kept_b, away_b, total_ref, bits[1], half_rows, index * units)


def block_kernel(mid_ref, keep_ref, core_ref, chip_ref, out_ref):
    total = mid_ref[...] + keep_ref[...]
    total = total + core_ref[...].astype(WIDE) + chip_ref[...].astype(WIDE)
    out_ref[...] = total.astype(LOW)


def attend_back_kernel(
    near_ref, far_ref, out_ref, total_ref, g0, g1, g2, g3, seg_row_ref, seg_col_ref,
    cos_ref, sin_ref, turned_ref, rows_near_ref, rows_far_ref,
    mixed_ref, keep_near_ref, keep_far_ref, away_near_ref, away_far_ref, gain_ref,
    keys_ref, values_ref, grad_ref, grad_keys_ref, grad_values_ref,
):
    length = seg_row_ref.shape[1]
    half_length = near_ref.shape[1]
    rows = g0.shape[1]
    width = g0.shape[0]
    heads = width // HD
    half = HD // 2
    scale = 1.0 / math.sqrt(HD)
    for place, ref in enumerate((g0, g1, g2, g3)):
        grad_ref[:, place * rows : (place + 1) * rows] = ref[...]

    def turn_back(total, first, at):
        cosine, sine = cos_ref[:, at], sin_ref[:, at]
        lower, upper = total[:half], total[half:]
        turned_lower = (lower * cosine + upper * sine).astype(LOW)
        turned_upper = (upper * cosine - lower * sine).astype(LOW)
        mixed_ref[pl.ds(first, half), at] = turned_lower
        mixed_ref[pl.ds(pl.multiple_of(first + half, half), half), at] = turned_upper

    def slab(head, first):
        return pl.ds(pl.multiple_of(first + head * HD, HD), HD)

    @pl.loop(0, heads)
    def _(head):
        here, keys_at, values_at = slab(head, 0), slab(head, width), slab(head, 2 * width)
        for place, ref in enumerate((near_ref, far_ref)):
            at = slice(place * half_length, (place + 1) * half_length)
            keys_ref[at, :] = ref[keys_at, :].T
            values_ref[at, :] = ref[values_at, :].T
        for tile in range(length // TILE):
            ref = near_ref if tile * TILE < half_length else far_ref
            first = (tile * TILE) % half_length
            at = slice(tile * TILE, (tile + 1) * TILE)
            column = jnp.concatenate([seg_col_ref[...]] * (TILE // seg_col_ref.shape[1]), 1)
            same = column == seg_row_ref[:, at]
            query = ref[here, first : first + TILE]
            grads = grad_ref[here, at]
            delta = jnp.sum(
                grads.astype(WIDE) * out_ref[here, at].astype(WIDE), 0, keepdims=True
            )
            scores = dot(keys_ref[...], query) - total_ref[head, :, at]
            probs = jnp.exp(jnp.where(same, scores, MASK_FLOOR))
            prob_grads = dot(values_ref[...], grads)
            score_grads = (probs * (prob_grads - delta)).astype(LOW)
            low = probs.astype(LOW)
            grad_query = dot(near_ref[keys_at, :], score_grads[:half_length])
            grad_query += dot(far_ref[keys_at, :], score_grads[half_length:])
            turn_back(grad_query * scale, pl.multiple_of(head * HD, HD), at)
            more_keys = dot(query, score_grads, 1, 1)
            more_values = dot(grads, low, 1, 1)
            if tile == 0:
                grad_keys_ref[...] = more_keys
                grad_values_ref[...] = more_values
            else:
                grad_keys_ref[...] += more_keys
                grad_values_ref[...] += more_values
        turn_back(
            grad_keys_ref[...], pl.multiple_of(width + head * HD, HD), slice(0, length)
        )
        mixed_ref[values_at, :] = grad_values_ref[...].astype(LOW)

    refs = (keep_near_ref, away_near_ref, keep_far_ref, away_far_ref)
    for place, ref in enumerate(refs):
        part = dot(mixed_ref[:, place * rows : (place + 1) * rows], turned_ref[...], 0, 0)
        ref[...] = part.astype(ref.dtype)
        normed = (rows_near_ref, rows_far_ref)[place // 2][
            place % 2 * rows : (place % 2 + 1) * rows, :
        ]
        more = jnp.sum(part * normed.astype(WIDE), 0, keepdims=True)
        gain_total = more if place == 0 else gain_total + more
    gain_ref[...] = gain_total


def qkv_grad_kernel(
    own_ref, normed_a, normed_b, mixed_ref, proj_keep, proj_core, proj_chip,
    kept_a, away_a, kept_b, away_b, total_ref, *, bits,
):
    half_length = normed_a.shape[1]
    local = proj_keep.shape[0]
    total = dot(normed_a[...], mixed_ref[:, :half_length], 1, 1)
    total += dot(normed_b[...], mixed_ref[:, half_length:], 1, 1)
    hold_blocks(total[:, : 2 * local], total_ref)
    store_blocks(own_ref, kept_a, away_a, total_ref, bits[0], 0, 0)
    proj = proj_keep[...] + proj_core[...].astype(WIDE) + proj_chip[...].astype(WIDE)
    hold_blocks(jnp.concatenate([total[:, 2 * local :], proj.T], 1), total_ref)
    store_blocks(own_ref, kept_b, away_b, total_ref, bits[1], 0, 0)


def finish_qkv_kernel(kept_a, came_a, kept_b, came_b, qkv_ref, proj_ref):
    local = proj_ref.shape[0]
    first = kept_a[...] + came_a[...].astype(WIDE)
    second = kept_b[...] + came_b[...].astype(WIDE)
    qkv_ref[0] = first[:, :local]
    qkv_ref[1] = first[:, local:]
    qkv_ref[2] = second[:, :local]
    proj_ref[...] = second[:, local:].T


def finish_wide_kernel(kept_a, came_a, kept_b, came_b, wide_ref, down_ref):
    units = down_ref.shape[0]
    half_rows = kept_a.shape[0]
    for place, (kept, came) in enumerate(((kept_a, came_a), (kept_b, came_b))):
        at = slice(place * half_rows, (place + 1) * half_rows)
        total = kept[...] + came[...].astype(WIDE)
        wide_ref[0, at, :] = total[:, :units]
        wide_ref[1, at, :] = total[:, units : 2 * units]
        down_ref[:, at] = total[:, 2 * units :].T


def last_kernel(x_ref, mid_ref, keep_ref, core_ref, chip_ref, gain_ref, out_ref):
    total = keep_ref[...] + core_ref[...].astype(WIDE) + chip_ref[...].astype(WIDE)
    hat, scale = normalise(x_ref[...].astype(WIDE))
    out_ref[...] = mid_ref[...] + normalise_back(total, hat, scale, gain_ref[...])


def output_kernel(act_a, act_b, down_ref, keep_near_ref, keep_far_ref, away_near_ref, away_far_ref):
    rows = keep_near_ref.shape[0]
    refs = (keep_near_ref, away_near_ref, keep_far_ref, away_far_ref)
    for place, ref in enumerate(refs):
        act = (act_a, act_b)[place // 2][place % 2 * rows : (place % 2 + 1) * rows, :]
        ref[...] = dot(act, down_ref[...]).astype(ref.dtype)


def reduce_parts(keep_far, away_far, away_near):
    came = swap(away_far, "tensor", 0)
    from_chip = swap((keep_far + came.astype(WIDE)).astype(LOW), "tensor", 1)
    return from_chip, swap(away_near, "tensor", 0)


def per_device(
    block_input,
    output_grad,
    segment_ids,
    positions,
    gain_one,
    gain_two,
    qkv_weight,
    proj_weight,
    wide_weight,
    down_weight,
):
    length = segment_ids.shape[1]
    rows, width = block_input.shape
    local = proj_weight.shape[0]
    heads = local // HD
    units = down_weight.shape[0]
    near = 2 * rows
    blocks = lax.axis_size("dp")
    own = lax.axis_index("dp").reshape(1)
    gain_a = gain_one.reshape(1, width)
    gain_b = gain_two.reshape(1, width)

    x_far = swap(block_input, "tensor", 1)
    x_core = swap(block_input, "tensor", 0)
    tables = ((HD // 2, length), WIDE)
    seg_row, seg_col, cosine, sine = call(
        functools.partial(prepare_kernel, count=lax.axis_size("tensor")),
        [((1, length), jnp.int32), ((length, 128), jnp.int32), tables, tables],
        lax.axis_index("tensor").reshape(1), segment_ids, positions,
        scalars=1,
    )
    turned = qkv_weight.reshape(width, 3 * local).T
    gate_w, up_w = wide_weight[:, 0].T, wide_weight[:, 1].T

    qkv_outs = [((width, near), LOW), ((near, width), LOW), ((3 * local, near), LOW)]
    qkv_flops = 2 * near * width * 3 * local
    normed_near, rows_near, mixed_near = call(
        functools.partial(qkv_kernel, offset=0), qkv_outs, block_input, x_core, gain_a, turned,
        cosine, sine, flops=qkv_flops,
    )
    x_both = swap(x_far, "tensor", 0)
    normed_far, rows_far, mixed_far = call(
        functools.partial(qkv_kernel, offset=near), qkv_outs, x_far, x_both, gain_a, turned,
        cosine, sine, flops=qkv_flops,
    )
    w0 = proj_weight
    w2 = swap(w0, "tensor", 1)
    w1 = swap(w0, "tensor", 0)
    w3 = swap(w2, "tensor", 0)
    g_far = swap(output_grad, "tensor", 1)
    g_core = swap(output_grad, "tensor", 0)
    g_both = swap(g_far, "tensor", 0)

    rows_wide, rows_low = ((rows, width), WIDE), ((rows, width), LOW)
    parts_outs = [rows_wide, rows_wide, rows_low, rows_low]
    head_parts = [((local, rows), LOW)] * 4
    attn, totals, a0, b1, b2, b3 = call(
        attend_kernel,
        [((local, length), LOW), ((heads, 1, length), WIDE)] + head_parts,
        mixed_near, mixed_far, seg_row, seg_col,
        scratch=[((heads, length, HD), LOW), ((local, length), LOW)],
        flops=16 * heads * length * length * HD,
    )
    a1 = exchange(b1, "tensor", 1)
    a2 = exchange(b2, "tensor", 2)
    a3 = exchange(b3, "tensor", 3)
    mid, n0 = call(
        middle_kernel, [rows_wide, rows_low],
        block_input, a0, a1, a2, a3, w0, w1, w2, w3, gain_b,
    )
    n2 = swap(n0, "tensor", 1)
    n1 = swap(n0, "tensor", 0)
    gain_row = ((1, width), WIDE)
    ff_outs = [((near, units), LOW)] * 3 + [rows_wide, rows_low, gain_row]
    ff_flops = 2 * near * width * units * 6
    dgate_near, dup_near, act_near, keep_near, away_near, gain_near = call(
        forward_kernel, ff_outs, n0, n1, output_grad, g_core, gate_w, up_w, down_weight,
        flops=ff_flops,
    )
    (wide_part,) = call(
        wide_near_kernel, [((3, width, units), WIDE)],
        n0, n1, output_grad, g_core, dgate_near, dup_near, act_near,
        flops=length * width * units * 3,
    )
    n3 = swap(n2, "tensor", 0)
    dgate_far, dup_far, act_far, keep_far, away_far, gain_far = call(
        forward_kernel, ff_outs, n2, n3, g_far, g_both, gate_w, up_w, down_weight,
        flops=ff_flops,
    )
    from_chip, from_core = reduce_parts(keep_far, away_far, away_near)
    grad_mid, m0, h0, e1, e2, e3 = call(
        middle_back_kernel, [rows_wide, rows_low] + head_parts,
        mid, output_grad, keep_near, from_core, from_chip, gain_b, w0, w1, w2, w3,
    )
    h1 = exchange(e1, "tensor", 1)
    h2 = exchange(e2, "tensor", 2)
    h3 = exchange(e3, "tensor", 3)
    head_wide, head_low = ((local, width), WIDE), ((local, width), LOW)
    proj_keep, proj_far, proj_away_near, proj_away_far = call(
        proj_grad_kernel, [head_wide, head_wide, head_low, head_low],
        a0, a1, a2, a3, m0, flops=2 * length * width * local,
    )
    proj_chip, proj_core = reduce_parts(proj_far, proj_away_far, proj_away_near)

    order = list(bits_of("dp"))
    turned_order = order[1:] + order[:1]
    firsts = (order[0], turned_order[0])
    half_rows = width // blocks // 2
    pieces = (blocks // 2, half_rows, 3 * units)
    kept_a, away_a, kept_b, away_b = call(
        functools.partial(wide_far_kernel, bits=firsts),
        [(pieces, WIDE), (pieces, LOW), (pieces, WIDE), (pieces, LOW)],
        own, n2, n3, g_far, g_both, dgate_far, dup_far, act_far, wide_part,
        scratch=[((blocks, width // blocks, units), WIDE)],
        scalars=1, flops=length * width * units * 3, limit=57,
    )
    first = scatter_rows(kept_a, away_a, order)
    second = scatter_rows(kept_b, away_b, turned_order)
    grad_wide, grad_down = call(
        finish_wide_kernel,
        [((2, width // blocks, units), WIDE), ((units, width // blocks), WIDE)],
        *first, *second,
    )

    out_near, out_far, out_away_near, out_away_far = call(
        output_kernel, parts_outs, act_near, act_far, down_weight,
        flops=2 * length * width * units,
    )
    out_chip, out_core = reduce_parts(out_far, out_away_far, out_away_near)
    (block_output,) = call(block_kernel, [rows_low], mid, out_near, out_core, out_chip)

    grad_mixed, keep_near, keep_far, away_near, away_far, gain_part_one = call(
        attend_back_kernel,
        [((3 * local, length), LOW)] + parts_outs + [gain_row],
        mixed_near, mixed_far, attn, totals, h0, h1, h2, h3, seg_row, seg_col,
        cosine, sine, turned, rows_near, rows_far,
        scratch=[((length, HD), LOW), ((length, HD), LOW), ((local, length), LOW),
                 ((HD, length), WIDE), ((HD, length), WIDE)],
        flops=40 * heads * length * length * HD,
    )
    from_chip, from_core = reduce_parts(keep_far, away_far, away_near)
    pieces = (blocks // 2, width // blocks, 2 * local)
    kept_a, away_a, kept_b, away_b = call(
        functools.partial(qkv_grad_kernel, bits=firsts),
        [(pieces, WIDE), (pieces, LOW), (pieces, WIDE), (pieces, LOW)],
        own, normed_near, normed_far, grad_mixed, proj_keep, proj_core, proj_chip,
        scalars=1, flops=2 * length * width * local * 4,
        scratch=[((blocks, width // blocks, 2 * local), WIDE)],
    )
    first = scatter_rows(kept_a, away_a, order)
    second = scatter_rows(kept_b, away_b, turned_order)
    grad_qkv, grad_proj = call(
        finish_qkv_kernel,
        [((3, width // blocks, local), WIDE), ((local, width // blocks), WIDE)],
        *first, *second,
    )
    grad_gains = sum_everywhere(
        jnp.concatenate([gain_part_one / gain_a, (gain_near + gain_far) / gain_b], 0)
    )
    (grad_input,) = call(
        last_kernel, [rows_wide],
        block_input, grad_mid, keep_near, from_core, from_chip, gain_a,
    )
    return (
        block_output,
        grad_input,
        jnp.transpose(grad_qkv, (1, 0, 2)),
        grad_proj,
        jnp.transpose(grad_wide, (1, 0, 2)),
        grad_down,
        grad_gains,
    )


def solution(mesh):
    placed = (
        P(("dp", "tensor"), None),
        P(("dp", "tensor"), None),
        P("dp", None),
        P("dp", None),
        P(),
        P(),
        P(None, None, "tensor"),
        P("tensor", None),
        P(None, None, "tensor"),
        P("tensor", None),
    )
    return jax.shard_map(
        per_device,
        mesh=mesh,
        in_specs=placed,
        out_specs=(
            P(("dp", "tensor"), None),
            P(("dp", "tensor"), None),
            P("dp", None, "tensor"),
            P("tensor", "dp"),
            P("dp", None, "tensor"),
            P("tensor", "dp"),
            P(),
        ),
        check_vma=False,
    )
```
